32 devices in a mesh: groups: 2 (over y), row: 4 (over x, core), col: 4 (over z).
Axes of the slice: x: 2, y: 2, z: 4, core: 2. Of those that a mesh axis runs over, the one named last changes fastest.
Arguments:
- features: bfloat16 [512, 256, 128], P(('groups', 'row'), 'col'), parts along dimension 0, may hold values from -6 to 6
- kernel_first: bfloat16 [3, 3, 128, 128], replicated, may hold values from -0.1875 to 0.1875
- bias_first: float32 [128], replicated, may hold values from -3 to 3
- mixer_first: bfloat16 [128, 128], replicated, may hold values from -0.5 to 0.5
- shift_first: float32 [128], replicated, may hold values from -3 to 3
- kernel_second: bfloat16 [3, 3, 128, 128], replicated, may hold values from -0.1875 to 0.1875
- bias_second: float32 [128], replicated, may hold values from -3 to 3
- mixer_second: bfloat16 [128, 128], replicated, may hold values from -0.5 to 0.5
- shift_second: float32 [128], replicated, may hold values from -3 to 3
Outputs:
- contacts: float32 [512, 256, 128], P(('groups', 'row'), 'col'), parts along dimension 0
The draws below stay inside these ranges and needn't reach their ends.
There are 2 independent parts, one for each index of `groups`. The reference program is written for one: setup_inputs(seed, part) draws one part's arguments, and reference() takes and returns one part's arrays. A program takes and returns all parts, laid end to end along the dimension named above; an argument that names none is the same for every part. Nothing has to cross between parts.
All inputs are finite; a program needn't handle non-finite values.
Results may differ from the reference program's by a relative error of at most 0.0045.
Values may be sent and summed in bfloat16 or wider, within the bound.
No kernel may reach another device: no remote copies, remote signals or barrier semaphores. Data moves between devices by JAX's collectives and lax.ppermute only.
A program may use at most 64 MiB of HBM per device.

```python
import jax
import jax.numpy as jnp

C = 128
L = 256


def block_scale(stream_key, shape, shards, smallest, high):
    def one(position, blocks):
        heights = jax.random.uniform(jax.random.fold_in(jax.random.fold_in(stream_key, 6), position), (blocks,), jnp.float32, smallest / len(shards), high / len(shards))
        return jnp.repeat(jnp.exp(heights), shape[position] // blocks).reshape((-1,) + (1,) * (len(shape) - position - 1))

    gain = one(*shards[0])
    for cut in shards[1:]:
        gain = gain * one(*cut)
    return gain


def noise(key, dims, width, reach, cuts=(), kind=jnp.bfloat16):
    values = width * jax.random.normal(key, dims, jnp.float32)
    if cuts:
        values = values * block_scale(key, dims, cuts, -0.22, 0.18)
    return jnp.clip(values, -reach, reach).astype(kind)


def setup_inputs(seed: int = 0, part: int = 0) -> dict:
    key_list = jax.random.split(jax.random.key(seed), 10)
    own_keys = jax.random.split(jax.random.fold_in(key_list[9], part), 10)
    features = noise(own_keys[0], (L, L, C), 1.0, 6.0, ((0, 4), (1, 4)))
    kernel_first = noise(key_list[1], (3, 3, C, C), (9 * C) ** -0.5, 0.1875)
    bias_first = noise(key_list[2], (C,), 0.5, 3.0, (), jnp.float32)
    mixer_first = noise(key_list[3], (C, C), C ** -0.5, 0.5)
    shift_first = noise(key_list[4], (C,), 0.5, 3.0, (), jnp.float32)
    kernel_second = noise(key_list[5], (3, 3, C, C), (9 * C) ** -0.5, 0.1875)
    bias_second = noise(key_list[6], (C,), 0.5, 3.0, (), jnp.float32)
    mixer_second = noise(key_list[7], (C, C), C ** -0.5, 0.5)
    shift_second = noise(key_list[8], (C,), 0.5, 3.0, (), jnp.float32)
    return {"features": features, "kernel_first": kernel_first, "bias_first": bias_first, "mixer_first": mixer_first, "shift_first": shift_first, "kernel_second": kernel_second, "bias_second": bias_second, "mixer_second": mixer_second, "shift_second": shift_second}


def run_block(source, kernel, conv_bias, mixer, mix_bias, spread):
    extent = source.shape[0]
    channels = source.shape[2]
    padded = jnp.pad(source, ((spread, spread), (spread, spread), (0, 0)))
    total = jnp.zeros((extent * extent, channels), jnp.float32)
    for tap_row in range(3):
        for tap_col in range(3):
            window = padded[tap_row * spread:tap_row * spread + extent, tap_col * spread:tap_col * spread + extent, :]
            total = total + jnp.dot(window.reshape(extent * extent, channels), kernel[tap_row, tap_col], preferred_element_type=jnp.float32)
    activated = jax.nn.relu(total + conv_bias).astype(jnp.bfloat16)
    mixed = jnp.dot(activated, mixer, preferred_element_type=jnp.float32) + mix_bias
    summed = (source.reshape(extent * extent, channels).astype(jnp.float32) + mixed).astype(jnp.bfloat16)
    summed = summed.reshape(extent, extent, channels).astype(jnp.float32)
    return jax.nn.relu((summed + jnp.swapaxes(summed, 0, 1)) * 0.5)


def reference(features, kernel_first, bias_first, mixer_first, shift_first, kernel_second, bias_second, mixer_second, shift_second):
    first = run_block(features, kernel_first, bias_first, mixer_first, shift_first, 2).astype(jnp.bfloat16)
    return run_block(first, kernel_second, bias_second, mixer_second, shift_second, 4)
```

```python
import functools

import jax
import jax.numpy as jnp
from jax import lax
from jax.experimental import pallas as pl
from jax.experimental.pallas import tpu as pltpu
from jax.sharding import PartitionSpec as P

BF16 = jnp.bfloat16
F32 = jnp.float32
NEAR = 2
FAR = 4
HALO = NEAR + FAR
PAD = 8
LEAD = 16


def mirror_routes(count):
    first, second = [], []
    for r in range(count):
        for c in range(count):
            if r == c:
                continue
            if r + c == count - 1:
                first.append((r * count + c, c * count + c))
                second.append((c * count + c, c * count + r))
            else:
                first.append((r * count + c, c * count + r))
    return first, second


def exchange(strips_low, strips_high, axis):
    count = lax.axis_size(axis)
    before = lax.ppermute(strips_high, axis, [(i, i + 1) for i in range(count - 1)])
    after = lax.ppermute(strips_low, axis, [(i + 1, i) for i in range(count - 1)])
    return before, after


def halo_pieces(tile):
    size = tile.shape[0]
    above, below = exchange(tile[:HALO], tile[size - HALO :], "row")
    low = jnp.concatenate([above[:, :PAD], tile[:, :PAD], below[:, :PAD]], axis=0)
    high = jnp.concatenate(
        [above[:, size - PAD :], tile[:, size - PAD :], below[:, size - PAD :]], axis=0
    )
    left, right = exchange(low, high, "col")
    return above, below, left, right


def paired_taps(kernel):
    channels = kernel.shape[2]
    flat = kernel.reshape(3, 3 * channels, channels)
    zero = jnp.zeros((1, 3 * channels, channels), kernel.dtype)
    near = jnp.concatenate([flat, zero], axis=0)
    far = jnp.concatenate([zero, flat], axis=0)
    return jnp.concatenate([near, far], axis=2).reshape(12 * channels, 2 * channels)


def twice(matrix):
    zero = jnp.zeros_like(matrix)
    return jnp.concatenate(
        [
            jnp.concatenate([matrix, zero], axis=1),
            jnp.concatenate([zero, matrix], axis=1),
        ],
        axis=0,
    )


def fill_edges(ext, above, below, left, right, size):
    rows = size + 2 * HALO
    ext[:, 0 : LEAD - PAD, :] = jnp.zeros((rows, LEAD - PAD, ext.shape[2]), BF16)
    tail = LEAD + size + PAD
    ext[:, tail:, :] = jnp.zeros((rows, ext.shape[1] - tail, ext.shape[2]), BF16)
    ext[0:HALO, LEAD : LEAD + size, :] = above[...]
    ext[HALO + size :, LEAD : LEAD + size, :] = below[...]
    ext[:, LEAD - PAD : LEAD, :] = left[...]
    ext[:, LEAD + size : tail, :] = right[...]


def near_block(wide, taps, bias, mix, shift, group, groups, width, channels):
    rows = groups * NEAR * width
    total = None
    for tap in range(4):
        part = wide[pl.ds(group + tap // 2, groups), tap % 2]
        part = part.reshape(rows, 3 * channels)
        product = jnp.dot(
            part,
            taps[tap * 3 * channels : (tap + 1) * 3 * channels, :],
            preferred_element_type=F32,
        )
        total = product if total is None else total + product
    active = jnp.maximum(total + bias[...], 0.0).astype(BF16)
    mixed = jnp.dot(active, mix[...], preferred_element_type=F32) + shift[...]
    return mixed


def split_pair(wide, mixed, half, group, groups, width, channels):
    center = wide[pl.ds(group + (1 if half else 0), groups), 0 if half else 1]
    center = center[..., channels : 2 * channels].astype(F32)
    part = mixed[:, half * channels : (half + 1) * channels]
    part = part.reshape(groups, NEAR, width, channels)
    return (center + part).astype(BF16)


def own_kernel(
    tile, above, below, left, right, taps, bias, mix, shift, out, ext, wide, *, steps
):
    size, channels = tile.shape[0], tile.shape[2]
    width = size + 2 * PAD
    fill_edges(ext, above, below, left, right, size)
    ext[HALO : HALO + size, LEAD : LEAD + size, :] = tile[...]
    widen(ext, wide, width, LEAD - PAD, NEAR, channels)
    total_groups = out.shape[0]
    groups = total_groups // steps

    def step(k, carry):
        group = k * groups
        mixed = near_block(
            wide, taps, bias, mix, shift, group, groups, width, channels
        )
        for half in range(2):
            out[pl.ds(group, groups), half] = split_pair(
                wide, mixed, half, group, groups, width, channels
            )
        return carry

    lax.fori_loop(0, steps, step, 0)


def widen(ext, wide, width, start, step, channels):
    for tap in range(3):
        begin = start + (tap - 1) * step
        lanes = slice(tap * channels, (tap + 1) * channels)
        if len(wide.shape) == 5:
            for row in range(ext.shape[0]):
                group, rest = divmod(row, 2 * step)
                wide[group, rest // step, rest % step, :, lanes] = ext[
                    row, begin : begin + width, :
                ]
        else:
            wide[:, :, lanes] = ext[:, begin : begin + width, :]


def main_kernel(*refs, chunks, steps, far_rows):
    count = len(chunks)
    own = refs[0]
    direct = refs[1 : 1 + count]
    relayed = refs[1 + count : 1 + 2 * count]
    (
        above,
        below,
        left,
        right,
        summed,
        taps,
        bias,
        mix,
        shift,
        far_taps,
        far_bias,
        far_mix,
        far_shift,
        out,
        ext,
        wide,
        first,
        far_wide,
        stage,
        sems,
    ) = refs[1 + 2 * count :]
    size, channels = own.shape[0], own.shape[2]
    width = size + 2 * PAD
    row, col = lax.axis_index("row"), lax.axis_index("col")
    last = lax.axis_size("row") - 1
    diagonal = row == col
    anti = jnp.logical_and(row + col == last, row != col)
    plain = jnp.logical_not(jnp.logical_or(diagonal, anti))

    fill_edges(ext, above, below, left, right, size)

    @pl.when(diagonal)
    def _():
        ext[HALO : HALO + size, LEAD : LEAD + size, :] = own[...]

    for sources, chosen in ((direct, plain), (relayed, anti)):

        @pl.when(chosen)
        def _(sources=sources):
            at = HALO
            for source in sources:
                ext[at : at + source.shape[0], LEAD : LEAD + size, :] = source[...]
                at += source.shape[0]

    widen(ext, wide, width, LEAD - PAD, NEAR, channels)
    total_groups = summed.shape[0]
    groups = total_groups // steps

    def step(k, carry):
        group = k * groups
        mixed = near_block(
            wide, taps, bias, mix, shift, group, groups, width, channels
        )
        for half in range(2):
            other = split_pair(wide, mixed, half, group, groups, width, channels)
            mean = (
                summed[pl.ds(group, groups), half].astype(F32) + other.astype(F32)
            ) * 0.5
            first[pl.ds(group, groups), half] = jnp.maximum(mean, 0.0).astype(BF16)
        return carry

    lax.fori_loop(0, steps, step, 0)

    edge = FAR // (2 * NEAR)

    @pl.when(row == 0)
    def _():
        first[0:edge] = jnp.zeros((edge,) + first.shape[1:], BF16)

    @pl.when(row == last)
    def _():
        first[total_groups - edge :] = jnp.zeros((edge,) + first.shape[1:], BF16)

    @pl.when(col == 0)
    def _():
        first[:, :, :, 0:PAD, :] = jnp.zeros(
            first.shape[:3] + (PAD, channels), BF16
        )

    @pl.when(col == last)
    def _():
        first[:, :, :, PAD + size :, :] = jnp.zeros(
            first.shape[:3] + (PAD, channels), BF16
        )

    for tap in range(3):
        begin = PAD + (tap - 1) * FAR
        far_wide[:, :, tap * channels : (tap + 1) * channels] = first[
            :, :, :, begin : begin + size, :
        ].reshape(size + 2 * FAR, size, channels)

    def copy(slot, base):
        return pltpu.make_async_copy(
            stage.at[slot], out.at[pl.ds(base, far_rows)], sems.at[slot]
        )

    blocks = size // far_rows

    def far_step(k, carry):
        slot = lax.rem(k, 2)
        base = k * far_rows

        @pl.when(k >= 2)
        def _():
            copy(slot, base - 2 * far_rows).wait()

        total = None
        for tap in range(3):
            part = far_wide[pl.ds(base + tap * FAR, far_rows)]
            part = part.reshape(far_rows * size, 3 * channels)
            product = jnp.dot(
                part,
                far_taps[tap * 3 * channels : (tap + 1) * 3 * channels, :],
                preferred_element_type=F32,
            )
            total = product if total is None else total + product
        active = jnp.maximum(total + far_bias[...], 0.0).astype(BF16)
        mixed = jnp.dot(active, far_mix[...], preferred_element_type=F32)
        center = far_wide[pl.ds(base + FAR, far_rows), :, channels : 2 * channels]
        center = center.reshape(far_rows * size, channels).astype(F32)
        value = jnp.maximum(center + far_shift[...] + 0.5 * mixed, 0.0)
        stage[slot] = value.reshape(far_rows, size, channels)
        copy(slot, base).start()
        return carry

    lax.fori_loop(0, blocks, far_step, 0)
    for k in range(max(blocks - 2, 0), blocks):
        copy(k % 2, k * far_rows).wait()


def body(
    features,
    kernel_first,
    bias_first,
    mixer_first,
    shift_first,
    kernel_second,
    bias_second,
    mixer_second,
    shift_second,
):
    size, _, channels = features.shape
    count = lax.axis_size("row")
    rows = size + 2 * HALO
    width = size + 2 * PAD
    groups = (size + 2 * FAR) // (2 * NEAR)
    pair = ("row", "col")
    direct_route, relay_route = mirror_routes(count)

    turned = jnp.swapaxes(features, 0, 1)
    cuts = (0, size * 3 // 16, size * 9 // 16, size)
    pieces = [turned[a:b] for a, b in zip(cuts[:-1], cuts[1:])]
    direct = [lax.ppermute(piece, pair, direct_route) for piece in pieces]
    relayed = [lax.ppermute(piece, pair, relay_route) for piece in direct]

    above, below, left, right = halo_pieces(features)

    row, col = lax.axis_index("row"), lax.axis_index("col")
    diagonal = row == col
    anti = row + col == count - 1
    mirrored = jnp.concatenate(
        [
            jnp.where(diagonal, piece, jnp.where(anti, late, early))
            for piece, early, late in zip(pieces, direct, relayed)
        ],
        axis=0,
    )
    m_above, m_below, m_left, m_right = halo_pieces(mirrored)

    whole = pl.BlockSpec(memory_space=pltpu.VMEM)
    double = lambda v: jnp.concatenate([v, v]).reshape(1, 2 * channels)
    mix_near = twice(mixer_first)
    ext = pltpu.VMEM((rows, 2 * LEAD + size, channels), BF16)
    wide = pltpu.VMEM(
        (rows // (2 * NEAR), 2, NEAR, width, 3 * channels), BF16
    )
    field = (groups, 2, NEAR, width, channels)
    near_flops = 2 * groups * 2 * NEAR * width * 10 * channels * channels
    summed = pl.pallas_call(
        functools.partial(own_kernel, steps=3),
        out_shape=jax.ShapeDtypeStruct(field, BF16),
        in_specs=[whole] * 9,
        out_specs=whole,
        scratch_shapes=[ext, wide],
        cost_estimate=pl.CostEstimate(
            flops=2 * near_flops, bytes_accessed=8 << 20, transcendentals=0
        ),
        name="own_block",
    )(
        features,
        above,
        below,
        left,
        right,
        paired_taps(kernel_first),
        double(bias_first),
        mix_near,
        double(shift_first),
    )

    straight = kernel_second.reshape(9 * channels, channels)
    crossed = jnp.swapaxes(kernel_second, 0, 1).reshape(9 * channels, channels)
    far_rows = 8
    return pl.pallas_call(
        functools.partial(main_kernel, chunks=pieces, steps=3, far_rows=far_rows),
        out_shape=jax.ShapeDtypeStruct(features.shape, F32),
        in_specs=[whole] * (1 + 2 * len(pieces) + 13),
        out_specs=pl.BlockSpec(memory_space=pl.ANY),
        scratch_shapes=[
            ext,
            wide,
            pltpu.VMEM(field, BF16),
            pltpu.VMEM((size + 2 * FAR, size, 3 * channels), BF16),
            pltpu.VMEM((2, far_rows, size, channels), F32),
            pltpu.SemaphoreType.DMA((2,)),
        ],
        cost_estimate=pl.CostEstimate(
            flops=4 * near_flops, bytes_accessed=16 << 20, transcendentals=0
        ),
        name="main_block",
    )(
        turned,
        *direct,
        *relayed,
        m_above,
        m_below,
        m_left,
        m_right,
        summed,
        paired_taps(jnp.swapaxes(kernel_first, 0, 1)),
        double(bias_first),
        mix_near,
        double(shift_first),
        jnp.concatenate([straight, crossed], axis=1),
        double(bias_second),
        jnp.concatenate([mixer_second, mixer_second], axis=0),
        shift_second.reshape(1, channels),
    )


def solution(mesh):
    return jax.shard_map(
        body,
        mesh=mesh,
        in_specs=(P(("groups", "row"), "col", None), P(), P(), P(), P(), P(), P(), P(), P()),
        out_specs=P(("groups", "row"), "col", None),
        check_vma=False,
    )
```

```python
import functools

import jax
import jax.numpy as jnp
from jax import lax
from jax.experimental import pallas as pl
from jax.experimental.pallas import tpu as pltpu
from jax.sharding import PartitionSpec as P

BF16 = jnp.bfloat16
F32 = jnp.float32
NEAR = 2
FAR = 4
HALO = NEAR + FAR
PAD = 8
LEAD = 16
GRANT = 28 << 20


def mirror_routes(count):
    straight, hop, onward = [], [], []
    for r in range(count):
        for c in range(count):
            if r == c:
                continue
            if r + c == count - 1:
                hop.append((r * count + c, c * count + c))
                onward.append((c * count + c, c * count + r))
            else:
                straight.append((r * count + c, c * count + r))
    return straight, hop, onward


def exchange(strips_low, strips_high, axis):
    count = lax.axis_size(axis)
    before = lax.ppermute(strips_high, axis, [(i, i + 1) for i in range(count - 1)])
    after = lax.ppermute(strips_low, axis, [(i + 1, i) for i in range(count - 1)])
    return before, after


def paired_taps(kernel):
    channels = kernel.shape[2]
    flat = kernel.reshape(3, 3 * channels, channels)
    zero = jnp.zeros((1, 3 * channels, channels), kernel.dtype)
    near = jnp.concatenate([flat, zero], axis=0)
    far = jnp.concatenate([zero, flat], axis=0)
    return jnp.concatenate([near, far], axis=2).reshape(12 * channels, 2 * channels)


def twice(matrix):
    zero = jnp.zeros_like(matrix)
    return jnp.concatenate(
        [
            jnp.concatenate([matrix, zero], axis=1),
            jnp.concatenate([zero, matrix], axis=1),
        ],
        axis=0,
    )


def fill_edges(ext, above, below, left, right, size):
    rows = size + 2 * HALO
    ext[:, 0 : LEAD - PAD, :] = jnp.zeros((rows, LEAD - PAD, ext.shape[2]), BF16)
    tail = LEAD + size + PAD
    ext[:, tail:, :] = jnp.zeros((rows, ext.shape[1] - tail, ext.shape[2]), BF16)
    ext[0:HALO, LEAD : LEAD + size, :] = above[...]
    ext[HALO + size :, LEAD : LEAD + size, :] = below[...]
    ext[:, LEAD - PAD : LEAD, :] = left[...]
    ext[:, LEAD + size : tail, :] = right[...]


def near_block(wide, taps, bias, mix, group, groups, width, channels):
    rows = groups * NEAR * width
    part = jnp.concatenate(
        [
            wide[pl.ds(group + tap // 2, groups), tap % 2].reshape(rows, 3 * channels)
            for tap in range(4)
        ],
        axis=1,
    )
    total = jnp.dot(part, taps[...], preferred_element_type=F32)
    active = jnp.maximum(total + bias[...], 0.0).astype(BF16)
    return jnp.dot(active, mix[...], preferred_element_type=F32)


def center_rows(wide, half, group, groups, channels):
    center = wide[pl.ds(group + half, groups), 1 - half]
    return center[..., channels : 2 * channels].astype(F32)


def widen(ext, wide, width, start, channels):
    for tap in range(3):
        begin = start + (tap - 1) * NEAR
        lanes = slice(tap * channels, (tap + 1) * channels)
        for row in range(ext.shape[0]):
            group, rest = divmod(row, 2 * NEAR)
            wide[group, rest // NEAR, rest % NEAR, :, lanes] = ext[
                row, begin : begin + width, :
            ]


def own_kernel(
    tile, above, below, left, right, taps, bias, mix, shift, out, ext, wide, *, steps
):
    size, channels = tile.shape[0], tile.shape[2]
    width = size + 2 * PAD
    fill_edges(ext, above, below, left, right, size)
    ext[HALO : HALO + size, LEAD : LEAD + size, :] = tile[...]
    widen(ext, wide, width, LEAD - PAD, channels)
    groups = out.shape[0] // steps

    def step(k, carry):
        group = k * groups
        mixed = near_block(wide, taps, bias, mix, group, groups, width, channels)
        for half in range(2):
            part = mixed[:, half * channels : (half + 1) * channels]
            part = part.reshape(groups, NEAR, width, channels)
            value = center_rows(wide, half, group, groups, channels) * 0.5 + part
            out[pl.ds(group, groups), half] = (value + shift[...]).astype(BF16)
        return carry

    lax.fori_loop(0, steps, step, 0)


def place_mirror(ext, frame, blocks, size):
    inner = size - 2 * PAD
    channels = ext.shape[2]
    top, low = HALO + PAD, HALO + PAD + inner
    lead, tail = LEAD + PAD, LEAD + PAD + inner
    band, side = PAD * size, inner * PAD
    ext[HALO:top, LEAD : LEAD + size, :] = frame[0:band].reshape(PAD, size, channels)
    ext[low : low + PAD, LEAD : LEAD + size, :] = frame[band : 2 * band].reshape(
        PAD, size, channels
    )
    ext[top:low, LEAD:lead, :] = frame[2 * band : 2 * band + side].reshape(
        inner, PAD, channels
    )
    ext[top:low, tail : tail + PAD, :] = frame[2 * band + side :].reshape(
        inner, PAD, channels
    )
    for block in blocks:
        rows = block.shape[0]
        ext[top : top + rows, lead:tail, :] = block[...]
        top += rows


def main_kernel(*refs, blocks, steps, far_rows):
    frame, own = refs[0], refs[1 : 1 + blocks]
    direct = refs[1 + blocks : 1 + 2 * blocks]
    relayed = refs[1 + 2 * blocks : 1 + 3 * blocks]
    (
        above,
        below,
        left,
        right,
        summed,
        taps,
        bias,
        mix,
        far_taps,
        far_bias,
        far_mix,
        far_shift,
        out,
        ext,
        wide,
        first,
        far_wide,
        stage,
        sems,
    ) = refs[1 + 3 * blocks :]
    size, channels = out.shape[0], out.shape[2]
    width = size + 2 * PAD
    row, col = lax.axis_index("row"), lax.axis_index("col")
    last = lax.axis_size("row") - 1
    diagonal = row == col
    anti = jnp.logical_and(row + col == last, row != col)
    plain = jnp.logical_not(jnp.logical_or(diagonal, anti))

    fill_edges(ext, above, below, left, right, size)
    for sources, chosen in ((own, diagonal), (direct, plain), (relayed, anti)):

        @pl.when(chosen)
        def _(sources=sources):
            place_mirror(ext, frame, sources, size)

    widen(ext, wide, width, LEAD - PAD, channels)
    total_groups = summed.shape[0]
    groups = total_groups // steps

    def step(k, carry):
        group = k * groups
        mixed = near_block(wide, taps, bias, mix, group, groups, width, channels)
        for half in range(2):
            part = mixed[:, half * channels : (half + 1) * channels]
            part = part.reshape(groups, NEAR, width, channels)
            value = center_rows(wide, half, group, groups, channels) * 0.5 + part
            value = value + summed[pl.ds(group, groups), half].astype(F32)
            first[pl.ds(group, groups), half] = jnp.maximum(value, 0.0).astype(BF16)
        return carry

    lax.fori_loop(0, steps, step, 0)

    edge = FAR // (2 * NEAR)

    @pl.when(row == 0)
    def _():
        first[0:edge] = jnp.zeros((edge,) + first.shape[1:], BF16)

    @pl.when(row == last)
    def _():
        first[total_groups - edge :] = jnp.zeros((edge,) + first.shape[1:], BF16)

    @pl.when(col == 0)
    def _():
        first[:, :, :, 0:PAD, :] = jnp.zeros(
            first.shape[:3] + (PAD, channels), BF16
        )

    @pl.when(col == last)
    def _():
        first[:, :, :, PAD + size :, :] = jnp.zeros(
            first.shape[:3] + (PAD, channels), BF16
        )

    for tap in range(3):
        begin = PAD + (tap - 1) * FAR
        far_wide[:, :, tap * channels : (tap + 1) * channels] = first[
            :, :, :, begin : begin + size, :
        ].reshape(size + 2 * FAR, size, channels)

    def copy(slot, base):
        return pltpu.make_async_copy(
            stage.at[slot], out.at[pl.ds(base, far_rows)], sems.at[slot]
        )

    count = size // far_rows

    def far_step(k, carry):
        slot = lax.rem(k, 2)
        base = k * far_rows

        @pl.when(k >= 2)
        def _():
            copy(slot, base - 2 * far_rows).wait()

        rows = far_rows * size
        part = jnp.concatenate(
            [
                far_wide[pl.ds(base + tap * FAR, far_rows)].reshape(rows, 3 * channels)
                for tap in range(3)
            ],
            axis=1,
        )
        total = jnp.dot(part, far_taps[...], preferred_element_type=F32)
        active = jnp.maximum(total + far_bias[...], 0.0).astype(BF16)
        mixed = jnp.dot(active, far_mix[...], preferred_element_type=F32)
        center = far_wide[pl.ds(base + FAR, far_rows), :, channels : 2 * channels]
        center = center.reshape(rows, channels).astype(F32)
        value = jnp.maximum(center + far_shift[...] + mixed, 0.0)
        stage[slot] = value.reshape(far_rows, size, channels)
        copy(slot, base).start()
        return carry

    lax.fori_loop(0, count, far_step, 0)
    for k in range(max(count - 2, 0), count):
        copy(k % 2, k * far_rows).wait()


def edge_strips(frame, size):
    inner = size - 2 * PAD
    channels = frame.shape[1]
    band, side = PAD * size, inner * PAD
    top = frame[0:band].reshape(PAD, size, channels)
    low = frame[band : 2 * band].reshape(PAD, size, channels)
    left = frame[2 * band : 2 * band + side].reshape(inner, PAD, channels)
    right = frame[2 * band + side :].reshape(inner, PAD, channels)
    left = jnp.concatenate([top[:, :PAD], left, low[:, :PAD]], axis=0)
    right = jnp.concatenate([top[:, size - PAD :], right, low[:, size - PAD :]], axis=0)
    return top[:HALO], low[PAD - HALO :], left, right


def halo_pieces(top, low, left, right):
    size = top.shape[1]
    above, below = exchange(top, low, "row")
    start = jnp.concatenate([above[:, :PAD], left, below[:, :PAD]], axis=0)
    end = jnp.concatenate(
        [above[:, size - PAD :], right, below[:, size - PAD :]], axis=0
    )
    before, after = exchange(start, end, "col")
    return above, below, before, after


def body(
    features,
    kernel_first,
    bias_first,
    mixer_first,
    shift_first,
    kernel_second,
    bias_second,
    mixer_second,
    shift_second,
):
    size, _, channels = features.shape
    count = lax.axis_size("row")
    rows = size + 2 * HALO
    width = size + 2 * PAD
    inner = size - 2 * PAD
    groups = (size + 2 * FAR) // (2 * NEAR)
    pair = ("row", "col")
    straight, hop, onward = mirror_routes(count)

    turned = jnp.swapaxes(features, 0, 1)
    frame = jnp.concatenate(
        [
            piece.reshape(-1, channels)
            for piece in (
                turned[:PAD],
                turned[size - PAD :],
                turned[PAD : size - PAD, :PAD],
                turned[PAD : size - PAD, size - PAD :],
            )
        ],
        axis=0,
    )
    inside = turned[PAD : size - PAD, PAD : size - PAD]
    cuts = (0, inner // 2, inner)
    blocks = [inside[a:b] for a, b in zip(cuts[:-1], cuts[1:])]

    hop_frame = lax.ppermute(frame, pair, hop)
    direct_frame = lax.ppermute(frame, pair, straight)
    direct = [lax.ppermute(block, pair, straight) for block in blocks]
    hops = [lax.ppermute(block, pair, hop) for block in blocks]
    relayed_frame = lax.ppermute(hop_frame, pair, onward)
    relayed = [lax.ppermute(block, pair, onward) for block in hops]

    tied, _, _ = lax.optimization_barrier((features, frame, inside))
    above, below, left, right = halo_pieces(
        tied[:HALO], tied[size - HALO :], tied[:, :PAD], tied[:, size - PAD :]
    )

    row, col = lax.axis_index("row"), lax.axis_index("col")
    diagonal = row == col
    anti = row + col == count - 1
    mirror_frame = jnp.where(
        diagonal, frame, jnp.where(anti, relayed_frame, direct_frame)
    )
    m_above, m_below, m_left, m_right = halo_pieces(*edge_strips(mirror_frame, size))

    whole = pl.BlockSpec(memory_space=pltpu.VMEM)
    double = lambda v: jnp.concatenate([v, v]).reshape(1, 2 * channels)
    half = lambda v: (v * 0.5).astype(v.dtype)
    mix_near = twice(half(mixer_first))
    ext = pltpu.VMEM((rows, 2 * LEAD + size, channels), BF16)
    wide = pltpu.VMEM(
        (rows // (2 * NEAR), 2, NEAR, width, 3 * channels), BF16
    )
    field = (groups, 2, NEAR, width, channels)
    near_flops = 2 * groups * 2 * NEAR * width * 10 * channels * channels
    summed = pl.pallas_call(
        functools.partial(own_kernel, steps=2),
        out_shape=jax.ShapeDtypeStruct(field, BF16),
        in_specs=[whole] * 9,
        out_specs=whole,
        scratch_shapes=[ext, wide],
        cost_estimate=pl.CostEstimate(
            flops=2 * near_flops, bytes_accessed=8 << 20, transcendentals=0
        ),
        compiler_params=pltpu.CompilerParams(vmem_limit_bytes=GRANT),
        name="own_block",
    )(
        features,
        above,
        below,
        left,
        right,
        paired_taps(kernel_first),
        double(bias_first),
        mix_near,
        shift_first.reshape(1, channels),
    )

    upright = kernel_second.reshape(9 * channels, channels)
    crossed = jnp.swapaxes(kernel_second, 0, 1).reshape(9 * channels, channels)
    far_rows = size // 4
    return pl.pallas_call(
        functools.partial(
            main_kernel, blocks=len(blocks), steps=2, far_rows=far_rows
        ),
        out_shape=jax.ShapeDtypeStruct(features.shape, F32),
        in_specs=[whole] * (1 + 3 * len(blocks) + 12),
        out_specs=pl.BlockSpec(memory_space=pl.ANY),
        scratch_shapes=[
            ext,
            wide,
            pltpu.VMEM(field, BF16),
            pltpu.VMEM((size + 2 * FAR, size, 3 * channels), BF16),
            pltpu.VMEM((2, far_rows, size, channels), F32),
            pltpu.SemaphoreType.DMA((2,)),
        ],
        cost_estimate=pl.CostEstimate(
            flops=4 * near_flops, bytes_accessed=16 << 20, transcendentals=0
        ),
        compiler_params=pltpu.CompilerParams(vmem_limit_bytes=GRANT),
        name="main_block",
    )(
        mirror_frame,
        *blocks,
        *direct,
        *relayed,
        m_above,
        m_below,
        m_left,
        m_right,
        summed,
        paired_taps(jnp.swapaxes(kernel_first, 0, 1)),
        double(bias_first),
        mix_near,
        jnp.concatenate([upright, crossed], axis=1),
        double(bias_second),
        half(jnp.concatenate([mixer_second, mixer_second], axis=0)),
        shift_second.reshape(1, channels),
    )


def solution(mesh):
    return jax.shard_map(
        body,
        mesh=mesh,
        in_specs=(P(("groups", "row"), "col", None), P(), P(), P(), P(), P(), P(), P(), P()),
        out_specs=P(("groups", "row"), "col", None),
        check_vma=False,
    )
```

```python
import functools

import jax
import jax.numpy as jnp
from jax import lax
from jax.experimental import pallas as pl
from jax.experimental.pallas import tpu as pltpu
from jax.sharding import PartitionSpec as P


BF16 = jnp.bfloat16
F32 = jnp.float32
NEAR = 2
FAR = 4
HALO = NEAR + FAR
PAD = 8
LEAD = 16
GRANT = 28 << 20


def mirror_routes(count):
    straight, hop, onward = [], [], []
    for r in range(count):
        for c in range(count):
            if r == c:
                continue
            if r + c == count - 1:
                hop.append((r * count + c, c * count + c))
                onward.append((c * count + c, c * count + r))
            else:
                straight.append((r * count + c, c * count + r))
    return straight, hop, onward


def paired_taps(kernel):
    channels = kernel.shape[2]
    flat = kernel.reshape(3, 3 * channels, channels)
    zero = jnp.zeros((1, 3 * channels, channels), kernel.dtype)
    near = jnp.concatenate([flat, zero], axis=0)
    far = jnp.concatenate([zero, flat], axis=0)
    return jnp.concatenate([near, far], axis=2).reshape(12 * channels, 2 * channels)


def twice(matrix):
    zero = jnp.zeros_like(matrix)
    return jnp.concatenate(
        [
            jnp.concatenate([matrix, zero], axis=1),
            jnp.concatenate([zero, matrix], axis=1),
        ],
        axis=0,
    )


def fill_edges(ext, above, below, left, right, size):
    rows = size + 2 * HALO
    ext[:, 0 : LEAD - PAD, :] = jnp.zeros((rows, LEAD - PAD, ext.shape[2]), BF16)
    tail = LEAD + size + PAD
    ext[:, tail:, :] = jnp.zeros((rows, ext.shape[1] - tail, ext.shape[2]), BF16)
    ext[0:HALO, LEAD : LEAD + size, :] = above[...]
    ext[HALO + size :, LEAD : LEAD + size, :] = below[...]
    ext[:, LEAD - PAD : LEAD, :] = left[...]
    ext[:, LEAD + size : tail, :] = right[...]


def near_block(wide, taps, bias, mix, group, groups, width, channels):
    rows = groups * NEAR * width
    part = jnp.concatenate(
        [
            wide[pl.ds(group + tap // 2, groups), tap % 2].reshape(rows, 3 * channels)
            for tap in range(4)
        ],
        axis=1,
    )
    total = jnp.dot(part, taps[...], preferred_element_type=F32)
    active = jnp.maximum(total + bias[...], 0.0).astype(BF16)
    return jnp.dot(active, mix[...], preferred_element_type=F32)


def center_rows(wide, half, group, groups, channels):
    center = wide[pl.ds(group + half, groups), 1 - half]
    return center[..., channels : 2 * channels].astype(F32)


def widen(ext, wide, width, start, channels):
    for tap in range(3):
        begin = start + (tap - 1) * NEAR
        lanes = slice(tap * channels, (tap + 1) * channels)
        for row in range(ext.shape[0]):
            group, rest = divmod(row, 2 * NEAR)
            wide[group, rest // NEAR, rest % NEAR, :, lanes] = ext[
                row, begin : begin + width, :
            ]


def own_kernel(
    tile, above, below, left, right, taps, bias, mix, shift, out, ext, wide, *, steps
):
    size, channels = tile.shape[0], tile.shape[2]
    width = size + 2 * PAD
    fill_edges(ext, *(edge.at[0] for edge in (above, below, left, right)), size)
    ext[HALO : HALO + size, LEAD : LEAD + size, :] = tile[...]
    widen(ext, wide, width, LEAD - PAD, channels)
    groups = out.shape[0] // steps

    def step(k, carry):
        group = k * groups
        mixed = near_block(wide, taps, bias, mix, group, groups, width, channels)
        for half in range(2):
            part = mixed[:, half * channels : (half + 1) * channels]
            part = part.reshape(groups, NEAR, width, channels)
            value = center_rows(wide, half, group, groups, channels) * 0.5 + part
            out[pl.ds(group, groups), half] = (value + shift[...]).astype(BF16)
        return carry

    lax.fori_loop(0, steps, step, 0)


def place_mirror(ext, frame, inside, size):
    channels = ext.shape[2]
    high = size - 2 * HALO
    band, side = HALO * size, high * PAD
    top, low = 2 * HALO, HALO + size - HALO
    lead, tail = LEAD + PAD, LEAD + size - PAD
    ext[HALO:top, LEAD : LEAD + size, :] = frame[0:band].reshape(HALO, size, channels)
    ext[low : low + HALO, LEAD : LEAD + size, :] = frame[band : 2 * band].reshape(
        HALO, size, channels
    )
    ext[top:low, LEAD:lead, :] = frame[2 * band : 2 * band + side].reshape(
        high, PAD, channels
    )
    ext[top:low, tail : tail + PAD, :] = frame[2 * band + side :].reshape(
        high, PAD, channels
    )
    ext[top:low, lead:tail, :] = inside[...]


def main_kernel(
    frame,
    own,
    direct,
    relayed,
    rows_above,
    rows_below,
    columns_left,
    columns_right,
    summed,
    taps,
    bias,
    mix,
    far_taps,
    far_bias,
    far_mix,
    far_shift,
    out,
    ext,
    wide,
    first,
    far_wide,
    stage,
    sems,
    *,
    steps,
    far_rows,
):
    size, channels = out.shape[0], out.shape[2]
    width = size + 2 * PAD
    row, col = lax.axis_index("row"), lax.axis_index("col")
    last = lax.axis_size("row") - 1
    diagonal = row == col
    anti = jnp.logical_and(row + col == last, row != col)
    plain = jnp.logical_not(jnp.logical_or(diagonal, anti))

    edges = (rows_above, rows_below, columns_left, columns_right)
    fill_edges(ext, *(edge.at[1] for edge in edges), size)
    for source, chosen in ((own, diagonal), (direct, plain), (relayed, anti)):

        @pl.when(chosen)
        def _(source=source):
            place_mirror(ext, frame, source, size)

    widen(ext, wide, width, LEAD - PAD, channels)
    total_groups = summed.shape[0]
    groups = total_groups // steps

    def step(k, carry):
        group = k * groups
        mixed = near_block(wide, taps, bias, mix, group, groups, width, channels)
        for half in range(2):
            part = mixed[:, half * channels : (half + 1) * channels]
            part = part.reshape(groups, NEAR, width, channels)
            value = center_rows(wide, half, group, groups, channels) * 0.5 + part
            value = value + summed[pl.ds(group, groups), half].astype(F32)
            first[pl.ds(group, groups), half] = jnp.maximum(value, 0.0).astype(BF16)
        return carry

    lax.fori_loop(0, steps, step, 0)

    edge = FAR // (2 * NEAR)

    @pl.when(row == 0)
    def _():
        first[0:edge] = jnp.zeros((edge,) + first.shape[1:], BF16)

    @pl.when(row == last)
    def _():
        first[total_groups - edge :] = jnp.zeros((edge,) + first.shape[1:], BF16)

    @pl.when(col == 0)
    def _():
        first[:, :, :, 0:PAD, :] = jnp.zeros(
            first.shape[:3] + (PAD, channels), BF16
        )

    @pl.when(col == last)
    def _():
        first[:, :, :, PAD + size :, :] = jnp.zeros(
            first.shape[:3] + (PAD, channels), BF16
        )

    for tap in range(3):
        begin = PAD + (tap - 1) * FAR
        far_wide[:, :, tap * channels : (tap + 1) * channels] = first[
            :, :, :, begin : begin + size, :
        ].reshape(size + 2 * FAR, size, channels)

    def copy(slot, base):
        return pltpu.make_async_copy(
            stage.at[slot], out.at[pl.ds(base, far_rows)], sems.at[slot]
        )

    count = size // far_rows

    def far_step(k, carry):
        slot = lax.rem(k, 2)
        base = k * far_rows

        @pl.when(k >= 2)
        def _():
            copy(slot, base - 2 * far_rows).wait()

        rows = far_rows * size
        part = jnp.concatenate(
            [
                far_wide[pl.ds(base + tap * FAR, far_rows)].reshape(rows, 3 * channels)
                for tap in range(3)
            ],
            axis=1,
        )
        total = jnp.dot(part, far_taps[...], preferred_element_type=F32)
        active = jnp.maximum(total + far_bias[...], 0.0).astype(BF16)
        mixed = jnp.dot(active, far_mix[...], preferred_element_type=F32)
        center = far_wide[pl.ds(base + FAR, far_rows), :, channels : 2 * channels]
        center = center.reshape(rows, channels).astype(F32)
        value = jnp.maximum(center + far_shift[...] + mixed, 0.0)
        stage[slot] = value.reshape(far_rows, size, channels)
        copy(slot, base).start()
        return carry

    lax.fori_loop(0, count, far_step, 0)
    for k in range(max(count - 2, 0), count):
        copy(k % 2, k * far_rows).wait()


def edge_strips(frame, size):
    high = size - 2 * HALO
    channels = frame.shape[1]
    band, side = HALO * size, high * PAD
    top = frame[0:band].reshape(HALO, size, channels)
    low = frame[band : 2 * band].reshape(HALO, size, channels)
    left = frame[2 * band : 2 * band + side].reshape(high, PAD, channels)
    right = frame[2 * band + side :].reshape(high, PAD, channels)
    left = jnp.concatenate([top[:, :PAD], left, low[:, :PAD]], axis=0)
    right = jnp.concatenate([top[:, size - PAD :], right, low[:, size - PAD :]], axis=0)
    return top, low, left, right


def exchange(strips_low, strips_high, axis):
    count = lax.axis_size(axis)
    before = lax.ppermute(strips_high, axis, [(i, i + 1) for i in range(count - 1)])
    after = lax.ppermute(strips_low, axis, [(i + 1, i) for i in range(count - 1)])
    return before, after


def halo_pieces(top, low, left, right):
    size = top.shape[2]
    above, below = exchange(top, low, "row")
    start = jnp.concatenate([above[:, :, :PAD], left, below[:, :, :PAD]], axis=1)
    end = jnp.concatenate(
        [above[:, :, size - PAD :], right, below[:, :, size - PAD :]], axis=1
    )
    before, after = exchange(start, end, "col")
    return above, below, before, after


def compute(
    features,
    kernel_first,
    bias_first,
    mixer_first,
    shift_first,
    kernel_second,
    bias_second,
    mixer_second,
    shift_second,
):
    size, _, channels = features.shape
    count = lax.axis_size("row")
    rows = size + 2 * HALO
    width = size + 2 * PAD
    groups = (size + 2 * FAR) // (2 * NEAR)
    pair = ("row", "col")
    straight, hop, onward = mirror_routes(count)

    def send(value, route):
        return lax.ppermute(value, pair, route)

    turned = jnp.swapaxes(features, 0, 1)
    inner = turned[HALO : size - HALO]
    frame = jnp.concatenate(
        [
            piece.reshape(-1, channels)
            for piece in (
                turned[:HALO],
                turned[size - HALO :],
                inner[:, :PAD],
                inner[:, size - PAD :],
            )
        ],
        axis=0,
    )
    inside = inner[:, PAD : size - PAD]
    direct_frame = send(frame, straight + hop)
    hop_inside = send(inside, hop)
    direct = send(inside, straight)
    relayed_frame = send(direct_frame, onward)
    relayed = send(hop_inside, onward)

    row, col = lax.axis_index("row"), lax.axis_index("col")
    diagonal = row == col
    anti = row + col == count - 1
    mirror_frame = jnp.where(
        diagonal, frame, jnp.where(anti, relayed_frame, direct_frame)
    )
    own_edges = (
        features[:HALO],
        features[size - HALO :],
        features[:, :PAD],
        features[:, size - PAD :],
    )
    edges = [
        jnp.stack(both) for both in zip(own_edges, edge_strips(mirror_frame, size))
    ]
    halos = halo_pieces(*edges)

    whole = pl.BlockSpec(memory_space=pltpu.VMEM)
    double = lambda v: jnp.concatenate([v, v]).reshape(1, 2 * channels)
    half = lambda v: (v * 0.5).astype(v.dtype)
    mix_near = twice(half(mixer_first))
    ext = pltpu.VMEM((rows, 2 * LEAD + size, channels), BF16)
    wide = pltpu.VMEM(
        (rows // (2 * NEAR), 2, NEAR, width, 3 * channels), BF16
    )
    field = (groups, 2, NEAR, width, channels)
    near_flops = 2 * groups * 2 * NEAR * width * 10 * channels * channels
    own_block = pl.pallas_call(
        functools.partial(own_kernel, steps=2),
        out_shape=jax.ShapeDtypeStruct(field, BF16),
        in_specs=[whole] * 9,
        out_specs=whole,
        scratch_shapes=[ext, wide],
        cost_estimate=pl.CostEstimate(
            flops=2 * near_flops, bytes_accessed=8 << 20, transcendentals=0
        ),
        compiler_params=pltpu.CompilerParams(vmem_limit_bytes=GRANT),
        name="own_block",
    )
    own_operands = (
        features,
        *halos,
        paired_taps(kernel_first),
        double(bias_first),
        mix_near,
        shift_first.reshape(1, channels),
    )
    summed = own_block(*own_operands)

    upright = kernel_second.reshape(9 * channels, channels)
    crossed = jnp.swapaxes(kernel_second, 0, 1).reshape(9 * channels, channels)
    far_rows = size // 4
    return pl.pallas_call(
        functools.partial(
            main_kernel, steps=2, far_rows=far_rows
        ),
        out_shape=jax.ShapeDtypeStruct(features.shape, F32),
        in_specs=[whole] * 16,
        out_specs=pl.BlockSpec(memory_space=pl.ANY),
        scratch_shapes=[
            ext,
            wide,
            pltpu.VMEM(field, BF16),
            pltpu.VMEM((size + 2 * FAR, size, 3 * channels), BF16),
            pltpu.VMEM((2, far_rows, size, channels), F32),
            pltpu.SemaphoreType.DMA((2,)),
        ],
        cost_estimate=pl.CostEstimate(
            flops=4 * near_flops, bytes_accessed=16 << 20, transcendentals=0
        ),
        compiler_params=pltpu.CompilerParams(vmem_limit_bytes=GRANT),
        name="main_block",
    )(
        mirror_frame,
        inside,
        direct,
        relayed,
        *halos,
        summed,
        paired_taps(jnp.swapaxes(kernel_first, 0, 1)),
        double(bias_first),
        mix_near,
        jnp.concatenate([upright, crossed], axis=1),
        double(bias_second),
        half(jnp.concatenate([mixer_second, mixer_second], axis=0)),
        shift_second.reshape(1, channels),
    )


def solution(mesh):
    return jax.shard_map(
        compute,
        mesh=mesh,
        in_specs=(P(("groups", "row"), "col", None), P(), P(), P(), P(), P(), P(), P(), P()),
        out_specs=P(("groups", "row"), "col", None),
        check_vma=False,
    )
```

```python
import functools

import jax
import jax.numpy as jnp
from jax import lax
from jax.experimental import pallas as pl
from jax.experimental.pallas import tpu as pltpu
from jax.sharding import PartitionSpec as P


BF16 = jnp.bfloat16
F32 = jnp.float32
NEAR = 2
FAR = 4
HALO = NEAR + FAR
PAD = 8
LEAD = 16
GRANT = 28 << 20


def mirror_routes(count):
    straight, hop, onward = [], [], []
    for r in range(count):
        for c in range(count):
            if r == c:
                continue
            if r + c == count - 1:
                hop.append((r * count + c, c * count + c))
                onward.append((c * count + c, c * count + r))
            else:
                straight.append((r * count + c, c * count + r))
    return straight, hop, onward


def paired_taps(kernel):
    channels = kernel.shape[2]
    flat = kernel.reshape(3, 3 * channels, channels)
    zero = jnp.zeros((1, 3 * channels, channels), kernel.dtype)
    near = jnp.concatenate([flat, zero], axis=0)
    far = jnp.concatenate([zero, flat], axis=0)
    return jnp.concatenate([near, far], axis=2).reshape(12 * channels, 2 * channels)


def twice(matrix):
    zero = jnp.zeros_like(matrix)
    return jnp.concatenate(
        [
            jnp.concatenate([matrix, zero], axis=1),
            jnp.concatenate([zero, matrix], axis=1),
        ],
        axis=0,
    )


def fill_edges(ext, above, below, left, right, size):
    rows = size + 2 * HALO
    ext[:, 0 : LEAD - PAD, :] = jnp.zeros((rows, LEAD - PAD, ext.shape[2]), BF16)
    tail = LEAD + size + PAD
    ext[:, tail:, :] = jnp.zeros((rows, ext.shape[1] - tail, ext.shape[2]), BF16)
    ext[0:HALO, LEAD : LEAD + size, :] = above[...]
    ext[HALO + size :, LEAD : LEAD + size, :] = below[...]
    ext[:, LEAD - PAD : LEAD, :] = left[...]
    ext[:, LEAD + size : tail, :] = right[...]


def near_block(wide, taps, bias, mix, group, groups, width, channels):
    rows = groups * NEAR * width
    part = jnp.concatenate(
        [
            wide[pl.ds(group + tap // 2, groups), tap % 2].reshape(rows, 3 * channels)
            for tap in range(4)
        ],
        axis=1,
    )
    total = jnp.dot(part, taps[...], preferred_element_type=F32)
    active = jnp.maximum(total + bias[...], 0.0).astype(BF16)
    return jnp.dot(active, mix[...], preferred_element_type=F32)


def center_rows(wide, half, group, groups, channels):
    center = wide[pl.ds(group + half, groups), 1 - half]
    return center[..., channels : 2 * channels].astype(F32)


def widen(ext, wide, width, start, channels):
    for tap in range(3):
        begin = start + (tap - 1) * NEAR
        lanes = slice(tap * channels, (tap + 1) * channels)
        for row in range(ext.shape[0]):
            group, rest = divmod(row, 2 * NEAR)
            wide[group, rest // NEAR, rest % NEAR, :, lanes] = ext[
                row, begin : begin + width, :
            ]


def own_kernel(
    tile, above, below, left, right, taps, bias, mix, shift, out, ext, wide, *, steps
):
    size, channels = tile.shape[0], tile.shape[2]
    width = size + 2 * PAD
    fill_edges(ext, above, below, left, right, size)
    ext[HALO : HALO + size, LEAD : LEAD + size, :] = tile[...]
    widen(ext, wide, width, LEAD - PAD, channels)
    groups = out.shape[0] // steps

    def step(k, carry):
        group = k * groups
        mixed = near_block(wide, taps, bias, mix, group, groups, width, channels)
        for half in range(2):
            part = mixed[:, half * channels : (half + 1) * channels]
            part = part.reshape(groups, NEAR, width, channels)
            value = center_rows(wide, half, group, groups, channels) * 0.5 + part
            out[pl.ds(group, groups), half] = (value + shift[...]).astype(BF16)
        return carry

    lax.fori_loop(0, steps, step, 0)


def place_mirror(ext, frame, inside, size):
    channels = ext.shape[2]
    high = size - 2 * HALO
    band, side = HALO * size, high * PAD
    top, low = 2 * HALO, HALO + size - HALO
    lead, tail = LEAD + PAD, LEAD + size - PAD
    ext[HALO:top, LEAD : LEAD + size, :] = frame[0:band].reshape(HALO, size, channels)
    ext[low : low + HALO, LEAD : LEAD + size, :] = frame[band : 2 * band].reshape(
        HALO, size, channels
    )
    ext[top:low, LEAD:lead, :] = frame[2 * band : 2 * band + side].reshape(
        high, PAD, channels
    )
    ext[top:low, tail : tail + PAD, :] = frame[2 * band + side :].reshape(
        high, PAD, channels
    )
    ext[top:low, lead:tail, :] = inside[...]


def main_kernel(
    frame,
    own,
    direct,
    relayed,
    rows_above,
    rows_below,
    columns_left,
    columns_right,
    summed,
    taps,
    bias,
    mix,
    far_taps,
    far_bias,
    far_mix,
    far_shift,
    out,
    ext,
    wide,
    first,
    far_wide,
    stage,
    sems,
    *,
    steps,
    far_rows,
):
    size, channels = out.shape[0], out.shape[2]
    width = size + 2 * PAD
    row, col = lax.axis_index("row"), lax.axis_index("col")
    last = lax.axis_size("row") - 1
    diagonal = row == col
    anti = jnp.logical_and(row + col == last, row != col)
    plain = jnp.logical_not(jnp.logical_or(diagonal, anti))

    edges = (rows_above, rows_below, columns_left, columns_right)
    fill_edges(ext, *edges, size)
    for source, chosen in ((own, diagonal), (direct, plain), (relayed, anti)):

        @pl.when(chosen)
        def _(source=source):
            place_mirror(ext, frame, source, size)

    widen(ext, wide, width, LEAD - PAD, channels)
    total_groups = summed.shape[0]
    groups = total_groups // steps

    def step(k, carry):
        group = k * groups
        mixed = near_block(wide, taps, bias, mix, group, groups, width, channels)
        for half in range(2):
            part = mixed[:, half * channels : (half + 1) * channels]
            part = part.reshape(groups, NEAR, width, channels)
            value = center_rows(wide, half, group, groups, channels) * 0.5 + part
            value = value + summed[pl.ds(group, groups), half].astype(F32)
            first[pl.ds(group, groups), half] = jnp.maximum(value, 0.0).astype(BF16)
        return carry

    lax.fori_loop(0, steps, step, 0)

    edge = FAR // (2 * NEAR)

    @pl.when(row == 0)
    def _():
        first[0:edge] = jnp.zeros((edge,) + first.shape[1:], BF16)

    @pl.when(row == last)
    def _():
        first[total_groups - edge :] = jnp.zeros((edge,) + first.shape[1:], BF16)

    @pl.when(col == 0)
    def _():
        first[:, :, :, 0:PAD, :] = jnp.zeros(
            first.shape[:3] + (PAD, channels), BF16
        )

    @pl.when(col == last)
    def _():
        first[:, :, :, PAD + size :, :] = jnp.zeros(
            first.shape[:3] + (PAD, channels), BF16
        )

    for tap in range(3):
        begin = PAD + (tap - 1) * FAR
        far_wide[:, :, tap * channels : (tap + 1) * channels] = first[
            :, :, :, begin : begin + size, :
        ].reshape(size + 2 * FAR, size, channels)

    def copy(slot, base):
        return pltpu.make_async_copy(
            stage.at[slot], out.at[pl.ds(base, far_rows)], sems.at[slot]
        )

    count = size // far_rows

    def far_step(k, carry):
        slot = lax.rem(k, 2)
        base = k * far_rows

        @pl.when(k >= 2)
        def _():
            copy(slot, base - 2 * far_rows).wait()

        rows = far_rows * size
        part = jnp.concatenate(
            [
                far_wide[pl.ds(base + tap * FAR, far_rows)].reshape(rows, 3 * channels)
                for tap in range(3)
            ],
            axis=1,
        )
        total = jnp.dot(part, far_taps[...], preferred_element_type=F32)
        active = jnp.maximum(total + far_bias[...], 0.0).astype(BF16)
        mixed = jnp.dot(active, far_mix[...], preferred_element_type=F32)
        center = far_wide[pl.ds(base + FAR, far_rows), :, channels : 2 * channels]
        center = center.reshape(rows, channels).astype(F32)
        value = jnp.maximum(center + far_shift[...] + mixed, 0.0)
        stage[slot] = value.reshape(far_rows, size, channels)
        copy(slot, base).start()
        return carry

    lax.fori_loop(0, count, far_step, 0)
    for k in range(max(count - 2, 0), count):
        copy(k % 2, k * far_rows).wait()


def edge_strips(frame, size):
    high = size - 2 * HALO
    channels = frame.shape[1]
    band, side = HALO * size, high * PAD
    top = frame[0:band].reshape(HALO, size, channels)
    low = frame[band : 2 * band].reshape(HALO, size, channels)
    left = frame[2 * band : 2 * band + side].reshape(high, PAD, channels)
    right = frame[2 * band + side :].reshape(high, PAD, channels)
    left = jnp.concatenate([top[:, :PAD], left, low[:, :PAD]], axis=0)
    right = jnp.concatenate([top[:, size - PAD :], right, low[:, size - PAD :]], axis=0)
    return top, low, left, right


def exchange(strips_low, strips_high, axis):
    count = lax.axis_size(axis)
    before = lax.ppermute(strips_high, axis, [(i, i + 1) for i in range(count - 1)])
    after = lax.ppermute(strips_low, axis, [(i + 1, i) for i in range(count - 1)])
    return before, after


def halo_pieces(top, low, left, right):
    size = top.shape[1]
    above, below = exchange(top, low, "row")
    start = jnp.concatenate([above[:, :PAD], left, below[:, :PAD]], axis=0)
    end = jnp.concatenate(
        [above[:, size - PAD :], right, below[:, size - PAD :]], axis=0
    )
    before, after = exchange(start, end, "col")
    return above, below, before, after


def compute(
    features,
    kernel_first,
    bias_first,
    mixer_first,
    shift_first,
    kernel_second,
    bias_second,
    mixer_second,
    shift_second,
):
    size, _, channels = features.shape
    count = lax.axis_size("row")
    rows = size + 2 * HALO
    width = size + 2 * PAD
    groups = (size + 2 * FAR) // (2 * NEAR)
    pair = ("row", "col")
    straight, hop, onward = mirror_routes(count)

    def send(value, route):
        return lax.ppermute(value, pair, route)

    turned = jnp.swapaxes(features, 0, 1)
    inner = turned[HALO : size - HALO]
    frame = jnp.concatenate(
        [
            piece.reshape(-1, channels)
            for piece in (
                turned[:HALO],
                turned[size - HALO :],
                inner[:, :PAD],
                inner[:, size - PAD :],
            )
        ],
        axis=0,
    )
    inside = inner[:, PAD : size - PAD]
    direct_frame = send(frame, straight + hop)
    hop_inside = send(inside, hop)
    direct = send(inside, straight)
    relayed_frame = send(direct_frame, onward)
    relayed = send(hop_inside, onward)

    row, col = lax.axis_index("row"), lax.axis_index("col")
    diagonal = row == col
    anti = row + col == count - 1
    mirror_frame = jnp.where(
        diagonal, frame, jnp.where(anti, relayed_frame, direct_frame)
    )
    own_halos = halo_pieces(
        features[:HALO],
        features[size - HALO :],
        features[:, :PAD],
        features[:, size - PAD :],
    )
    halos = halo_pieces(*edge_strips(mirror_frame, size))

    whole = pl.BlockSpec(memory_space=pltpu.VMEM)
    double = lambda v: jnp.concatenate([v, v]).reshape(1, 2 * channels)
    half = lambda v: (v * 0.5).astype(v.dtype)
    mix_near = twice(half(mixer_first))
    ext = pltpu.VMEM((rows, 2 * LEAD + size, channels), BF16)
    wide = pltpu.VMEM(
        (rows // (2 * NEAR), 2, NEAR, width, 3 * channels), BF16
    )
    field = (groups, 2, NEAR, width, channels)
    near_flops = 2 * groups * 2 * NEAR * width * 10 * channels * channels
    own_block = pl.pallas_call(
        functools.partial(own_kernel, steps=2),
        out_shape=jax.ShapeDtypeStruct(field, BF16),
        in_specs=[whole] * 9,
        out_specs=whole,
        scratch_shapes=[ext, wide],
        cost_estimate=pl.CostEstimate(
            flops=2 * near_flops, bytes_accessed=8 << 20, transcendentals=0
        ),
        compiler_params=pltpu.CompilerParams(vmem_limit_bytes=GRANT),
        name="own_block",
    )
    own_operands = (
        features,
        *own_halos,
        paired_taps(kernel_first),
        double(bias_first),
        mix_near,
        shift_first.reshape(1, channels),
    )
    summed = own_block(*own_operands)

    upright = kernel_second.reshape(9 * channels, channels)
    crossed = jnp.swapaxes(kernel_second, 0, 1).reshape(9 * channels, channels)
    far_rows = size // 4
    return pl.pallas_call(
        functools.partial(
            main_kernel, steps=2, far_rows=far_rows
        ),
        out_shape=jax.ShapeDtypeStruct(features.shape, F32),
        in_specs=[whole] * 16,
        out_specs=pl.BlockSpec(memory_space=pl.ANY),
        scratch_shapes=[
            ext,
            wide,
            pltpu.VMEM(field, BF16),
            pltpu.VMEM((size + 2 * FAR, size, 3 * channels), BF16),
            pltpu.VMEM((2, far_rows, size, channels), F32),
            pltpu.SemaphoreType.DMA((2,)),
        ],
        cost_estimate=pl.CostEstimate(
            flops=4 * near_flops, bytes_accessed=16 << 20, transcendentals=0
        ),
        compiler_params=pltpu.CompilerParams(vmem_limit_bytes=GRANT),
        name="main_block",
    )(
        mirror_frame,
        inside,
        direct,
        relayed,
        *halos,
        summed,
        paired_taps(jnp.swapaxes(kernel_first, 0, 1)),
        double(bias_first),
        mix_near,
        jnp.concatenate([upright, crossed], axis=1),
        double(bias_second),
        half(jnp.concatenate([mixer_second, mixer_second], axis=0)),
        shift_second.reshape(1, channels),
    )


def solution(mesh):
    return jax.shard_map(
        compute,
        mesh=mesh,
        in_specs=(P(("groups", "row"), "col", None), P(), P(), P(), P(), P(), P(), P(), P()),
        out_specs=P(("groups", "row"), "col", None),
        check_vma=False,
    )
```

```python
import functools

import jax
import jax.numpy as jnp
from jax import lax
from jax.experimental import pallas as pl
from jax.experimental.pallas import tpu as pltpu
from jax.sharding import PartitionSpec as P


BF16 = jnp.bfloat16
F32 = jnp.float32
NEAR = 2
FAR = 4
HALO = NEAR + FAR
PAD = 8
LEAD = 16
GRANT = 28 << 20


def mirror_routes(count):
    straight, hop, onward = [], [], []
    for r in range(count):
        for c in range(count):
            if r == c:
                continue
            if r + c == count - 1:
                hop.append((r * count + c, c * count + c))
                onward.append((c * count + c, c * count + r))
            else:
                straight.append((r * count + c, c * count + r))
    return straight, hop, onward


def place_pairs(out, kernel, turned):
    channels = kernel.shape[2]
    for tap in range(4):
        for half in range(2):
            for side in range(3):
                begin = (3 * tap + side) * channels
                target = out.at[
                    begin : begin + channels, half * channels : (half + 1) * channels
                ]
                down = tap - half
                if 0 <= down < 3:
                    place = (side, down) if turned else (down, side)
                    target[...] = kernel[place]
                else:
                    target[...] = jnp.zeros((channels, channels), BF16)


def place_both(out, kernel):
    channels = kernel.shape[2]
    for down in range(3):
        for side in range(3):
            begin = (3 * down + side) * channels
            out[begin : begin + channels, :channels] = kernel[down, side]
            out[begin : begin + channels, channels:] = kernel[side, down]


def place_twice(out, matrix):
    channels = matrix.shape[0]
    value = (matrix[...].astype(F32) * 0.5).astype(BF16)
    zero = jnp.zeros((channels, channels), BF16)
    out[:channels, :channels] = value
    out[channels:, channels:] = value
    out[:channels, channels:] = zero
    out[channels:, :channels] = zero


def fill_edges(ext, row_near, row_far, col_near, col_far, size):
    rows = size + 2 * HALO
    tail = LEAD + size + PAD
    ext[:, 0 : LEAD - PAD, :] = jnp.zeros((rows, LEAD - PAD, ext.shape[2]), BF16)
    ext[:, tail:, :] = jnp.zeros((rows, ext.shape[1] - tail, ext.shape[2]), BF16)

    def place(axis, near, far, low, high):
        even = lax.rem(lax.axis_index(axis), 2) == 0

        @pl.when(even)
        def _():
            low[...] = far[...]
            high[...] = near[...]

        @pl.when(jnp.logical_not(even))
        def _():
            low[...] = near[...]
            high[...] = far[...]

    within = slice(LEAD, LEAD + size)
    place(
        "row", row_near, row_far, ext.at[0:HALO, within], ext.at[HALO + size :, within]
    )
    place(
        "col",
        col_near,
        col_far,
        ext.at[:, LEAD - PAD : LEAD],
        ext.at[:, LEAD + size : tail],
    )


def near_block(wide, taps, bias, mix, group, groups, width, channels):
    rows = groups * NEAR * width
    part = jnp.concatenate(
        [
            wide[pl.ds(group + tap // 2, groups), tap % 2].reshape(rows, 3 * channels)
            for tap in range(4)
        ],
        axis=1,
    )
    total = jnp.dot(part, taps[...], preferred_element_type=F32)
    both = jnp.concatenate([bias[...], bias[...]], axis=1)
    active = jnp.maximum(total + both, 0.0).astype(BF16)
    return jnp.dot(active, mix[...], preferred_element_type=F32)


def center_rows(wide, half, group, groups, channels):
    center = wide[pl.ds(group + half, groups), 1 - half]
    return center[..., channels : 2 * channels].astype(F32)


def widen(ext, wide, width, start, channels):
    for tap in range(3):
        begin = start + (tap - 1) * NEAR
        lanes = slice(tap * channels, (tap + 1) * channels)
        for row in range(ext.shape[0]):
            group, rest = divmod(row, 2 * NEAR)
            wide[group, rest // NEAR, rest % NEAR, :, lanes] = ext[
                row, begin : begin + width, :
            ]


def own_kernel(
    tile,
    row_near,
    row_far,
    col_near,
    col_far,
    kernel,
    bias,
    mixer,
    shift,
    far_kernel,
    far_mixer,
    out,
    mirror_taps,
    mix,
    far_taps,
    far_mix,
    ext,
    wide,
    taps,
    *,
    steps,
):
    place_pairs(taps, kernel, False)
    place_pairs(mirror_taps, kernel, True)
    place_twice(mix, mixer)
    place_both(far_taps, far_kernel)
    place_twice(far_mix, far_mixer)
    size, channels = tile.shape[0], tile.shape[2]
    width = size + 2 * PAD
    fill_edges(ext, row_near, row_far, col_near, col_far, size)
    ext[HALO : HALO + size, LEAD : LEAD + size, :] = tile[...]
    widen(ext, wide, width, LEAD - PAD, channels)
    groups = out.shape[0] // steps

    def step(k, carry):
        group = k * groups
        mixed = near_block(wide, taps, bias, mix, group, groups, width, channels)
        for half in range(2):
            part = mixed[:, half * channels : (half + 1) * channels]
            part = part.reshape(groups, NEAR, width, channels)
            value = center_rows(wide, half, group, groups, channels) * 0.5 + part
            out[pl.ds(group, groups), half] = (value + shift[...]).astype(BF16)
        return carry

    lax.fori_loop(0, steps, step, 0)


def place_mirror(ext, frame, inside, size):
    channels = ext.shape[2]
    high = size - 2 * HALO
    band, side = HALO * size, high * PAD
    top, low = 2 * HALO, HALO + size - HALO
    lead, tail = LEAD + PAD, LEAD + size - PAD
    ext[HALO:top, LEAD : LEAD + size, :] = frame[0:band].reshape(HALO, size, channels)
    ext[low : low + HALO, LEAD : LEAD + size, :] = frame[band : 2 * band].reshape(
        HALO, size, channels
    )
    ext[top:low, LEAD:lead, :] = frame[2 * band : 2 * band + side].reshape(
        high, PAD, channels
    )
    ext[top:low, tail : tail + PAD, :] = frame[2 * band + side :].reshape(
        high, PAD, channels
    )
    ext[top:low, lead:tail, :] = inside[...]


def main_kernel(
    frame,
    own,
    direct,
    relayed,
    row_near,
    row_far,
    col_near,
    col_far,
    summed,
    taps,
    bias,
    mix,
    far_taps,
    far_bias,
    far_mix,
    far_shift,
    out,
    ext,
    wide,
    first,
    far_wide,
    stage,
    sems,
    *,
    steps,
    far_rows,
):
    size, channels = out.shape[0], out.shape[2]
    width = size + 2 * PAD
    row, col = lax.axis_index("row"), lax.axis_index("col")
    last = lax.axis_size("row") - 1
    diagonal = row == col
    anti = jnp.logical_and(row + col == last, row != col)
    plain = jnp.logical_not(jnp.logical_or(diagonal, anti))

    fill_edges(ext, row_near, row_far, col_near, col_far, size)
    for source, chosen in ((own, diagonal), (direct, plain), (relayed, anti)):

        @pl.when(chosen)
        def _(source=source):
            place_mirror(ext, frame, source, size)

    widen(ext, wide, width, LEAD - PAD, channels)
    total_groups = summed.shape[0]
    groups = total_groups // steps

    def step(k, carry):
        group = k * groups
        mixed = near_block(wide, taps, bias, mix, group, groups, width, channels)
        for half in range(2):
            part = mixed[:, half * channels : (half + 1) * channels]
            part = part.reshape(groups, NEAR, width, channels)
            value = center_rows(wide, half, group, groups, channels) * 0.5 + part
            value = value + summed[pl.ds(group, groups), half].astype(F32)
            first[pl.ds(group, groups), half] = jnp.maximum(value, 0.0).astype(BF16)
        return carry

    lax.fori_loop(0, steps, step, 0)

    edge = FAR // (2 * NEAR)

    @pl.when(row == 0)
    def _():
        first[0:edge] = jnp.zeros((edge,) + first.shape[1:], BF16)

    @pl.when(row == last)
    def _():
        first[total_groups - edge :] = jnp.zeros((edge,) + first.shape[1:], BF16)

    @pl.when(col == 0)
    def _():
        first[:, :, :, 0:PAD, :] = jnp.zeros(
            first.shape[:3] + (PAD, channels), BF16
        )

    @pl.when(col == last)
    def _():
        first[:, :, :, PAD + size :, :] = jnp.zeros(
            first.shape[:3] + (PAD, channels), BF16
        )

    for tap in range(3):
        begin = PAD + (tap - 1) * FAR
        far_wide[:, :, tap * channels : (tap + 1) * channels] = first[
            :, :, :, begin : begin + size, :
        ].reshape(size + 2 * FAR, size, channels)

    def copy(slot, base):
        return pltpu.make_async_copy(
            stage.at[slot], out.at[pl.ds(base, far_rows)], sems.at[slot]
        )

    count = size // far_rows

    def far_step(k, carry):
        slot = lax.rem(k, 2)
        base = k * far_rows

        @pl.when(k >= 2)
        def _():
            copy(slot, base - 2 * far_rows).wait()

        rows = far_rows * size
        part = jnp.concatenate(
            [
                far_wide[pl.ds(base + tap * FAR, far_rows)].reshape(rows, 3 * channels)
                for tap in range(3)
            ],
            axis=1,
        )
        total = jnp.dot(part, far_taps[...], preferred_element_type=F32)
        active = jnp.maximum(total[:, :channels] + far_bias[...], 0.0)
        active = active + jnp.maximum(total[:, channels:] + far_bias[...], 0.0)
        active = active.astype(BF16)
        active = jnp.concatenate([active[: rows // 2], active[rows // 2 :]], axis=1)
        mixed = jnp.dot(active, far_mix[...], preferred_element_type=F32)
        mixed = jnp.concatenate([mixed[:, :channels], mixed[:, channels:]], axis=0)
        center = far_wide[pl.ds(base + FAR, far_rows), :, channels : 2 * channels]
        center = center.reshape(rows, channels).astype(F32)
        value = jnp.maximum(center + far_shift[...] + mixed, 0.0)
        stage[slot] = value.reshape(far_rows, size, channels)
        copy(slot, base).start()
        return carry

    lax.fori_loop(0, count, far_step, 0)
    for k in range(max(count - 2, 0), count):
        copy(k % 2, k * far_rows).wait()


def edge_strips(frame, size):
    high = size - 2 * HALO
    channels = frame.shape[1]
    band, side = HALO * size, high * PAD
    top = frame[0:band].reshape(HALO, size, channels)
    low = frame[band : 2 * band].reshape(HALO, size, channels)
    left = frame[2 * band : 2 * band + side].reshape(high, PAD, channels)
    right = frame[2 * band + side :].reshape(high, PAD, channels)
    left = jnp.concatenate([top[:, :PAD], left, low[:, :PAD]], axis=0)
    right = jnp.concatenate([top[:, size - PAD :], right, low[:, size - PAD :]], axis=0)
    return top, low, left, right


def exchange(low, high, axis):
    count = lax.axis_size(axis)
    even = lax.axis_index(axis) % 2 == 0

    def swap(first, value):
        pairs = [(i, i + 1) for i in range(first, count - 1, 2)]
        return lax.ppermute(value, axis, pairs + [(j, i) for i, j in pairs])

    near = swap(0, jnp.where(even, high, low))
    far = swap(1, jnp.where(even, low, high))
    return near, far


def halo_pieces(top, low, left, right):
    size = top.shape[1]
    near, far = exchange(top, low, "row")
    even = lax.axis_index("row") % 2 == 0
    above, below = jnp.where(even, far, near), jnp.where(even, near, far)
    start = jnp.concatenate([above[:, :PAD], left, below[:, :PAD]], axis=0)
    end = jnp.concatenate(
        [above[:, size - PAD :], right, below[:, size - PAD :]], axis=0
    )
    return (near, far) + exchange(start, end, "col")


def compute(
    features,
    kernel_first,
    bias_first,
    mixer_first,
    shift_first,
    kernel_second,
    bias_second,
    mixer_second,
    shift_second,
):
    size, _, channels = features.shape
    count = lax.axis_size("row")
    rows = size + 2 * HALO
    width = size + 2 * PAD
    groups = (size + 2 * FAR) // (2 * NEAR)
    pair = ("row", "col")
    straight, hop, onward = mirror_routes(count)

    def send(value, route):
        return lax.ppermute(value, pair, route)

    turned = jnp.swapaxes(features, 0, 1)
    inner = turned[HALO : size - HALO]
    frame = jnp.concatenate(
        [
            piece.reshape(-1, channels)
            for piece in (
                turned[:HALO],
                turned[size - HALO :],
                inner[:, :PAD],
                inner[:, size - PAD :],
            )
        ],
        axis=0,
    )
    inside = inner[:, PAD : size - PAD]
    direct_frame = send(frame, straight + hop)
    hop_inside = send(inside, hop)
    direct = send(inside, straight)
    relayed_frame = send(direct_frame, onward)
    relayed = send(hop_inside, onward)

    row, col = lax.axis_index("row"), lax.axis_index("col")
    diagonal = row == col
    anti = row + col == count - 1
    mirror_frame = jnp.where(
        diagonal, frame, jnp.where(anti, relayed_frame, direct_frame)
    )
    own_halos = halo_pieces(
        features[:HALO],
        features[size - HALO :],
        features[:, :PAD],
        features[:, size - PAD :],
    )
    halos = halo_pieces(*edge_strips(mirror_frame, size))

    whole = pl.BlockSpec(memory_space=pltpu.VMEM)
    line = lambda v: v.reshape(1, channels)
    ext = pltpu.VMEM((rows, 2 * LEAD + size, channels), BF16)
    wide = pltpu.VMEM(
        (rows // (2 * NEAR), 2, NEAR, width, 3 * channels), BF16
    )
    field = (groups, 2, NEAR, width, channels)
    pairs = (12 * channels, 2 * channels)
    square = (2 * channels, 2 * channels)
    near_flops = 2 * groups * 2 * NEAR * width * 10 * channels * channels
    own_block = pl.pallas_call(
        functools.partial(own_kernel, steps=2),
        out_shape=[
            jax.ShapeDtypeStruct(shape, BF16)
            for shape in (field, pairs, square, (9 * channels, 2 * channels), square)
        ],
        in_specs=[whole] * 11,
        out_specs=[whole] * 5,
        scratch_shapes=[ext, wide, pltpu.VMEM(pairs, BF16)],
        cost_estimate=pl.CostEstimate(
            flops=2 * near_flops, bytes_accessed=8 << 20, transcendentals=0
        ),
        compiler_params=pltpu.CompilerParams(vmem_limit_bytes=GRANT),
        name="own_block",
    )
    own_operands = (
        features,
        *own_halos,
        kernel_first,
        line(bias_first),
        mixer_first,
        line(shift_first),
        kernel_second,
        mixer_second,
    )
    summed, taps, mix, far_taps, far_mix = own_block(*own_operands)

    far_rows = size // 4
    return pl.pallas_call(
        functools.partial(main_kernel, steps=1, far_rows=far_rows),
        out_shape=jax.ShapeDtypeStruct(features.shape, F32),
        in_specs=[whole] * 16,
        out_specs=pl.BlockSpec(memory_space=pl.ANY),
        scratch_shapes=[
            ext,
            wide,
            pltpu.VMEM(field, BF16),
            pltpu.VMEM((size + 2 * FAR, size, 3 * channels), BF16),
            pltpu.VMEM((2, far_rows, size, channels), F32),
            pltpu.SemaphoreType.DMA((2,)),
        ],
        cost_estimate=pl.CostEstimate(
            flops=4 * near_flops, bytes_accessed=16 << 20, transcendentals=0
        ),
        compiler_params=pltpu.CompilerParams(vmem_limit_bytes=GRANT),
        name="main_block",
    )(
        mirror_frame,
        inside,
        direct,
        relayed,
        *halos,
        summed,
        taps,
        line(bias_first),
        mix,
        far_taps,
        line(bias_second),
        far_mix,
        line(shift_second),
    )


def solution(mesh):
    return jax.shard_map(
        compute,
        mesh=mesh,
        in_specs=(P(("groups", "row"), "col", None), P(), P(), P(), P(), P(), P(), P(), P()),
        out_specs=P(("groups", "row"), "col", None),
        check_vma=False,
    )
```

```python
import functools

import jax
import jax.numpy as jnp
from jax import lax
from jax.experimental import pallas as pl
from jax.experimental.pallas import tpu as pltpu
from jax.sharding import PartitionSpec as P


BF16 = jnp.bfloat16
F32 = jnp.float32
NEAR = 2
FAR = 4
HALO = NEAR + FAR
PAD = 8
LEAD = 16
GRANT = 28 << 20


def mirror_routes(count):
    straight, hop, onward = [], [], []
    for r in range(count):
        for c in range(count):
            if r == c:
                continue
            if r + c == count - 1:
                hop.append((r * count + c, c * count + c))
                onward.append((c * count + c, c * count + r))
            else:
                straight.append((r * count + c, c * count + r))
    return straight, hop, onward


def place_pairs(out, kernel, turned):
    channels = kernel.shape[2]
    for tap in range(4):
        for half in range(2):
            for side in range(3):
                begin = (3 * tap + side) * channels
                target = out.at[
                    begin : begin + channels, half * channels : (half + 1) * channels
                ]
                down = tap - half
                if 0 <= down < 3:
                    place = (side, down) if turned else (down, side)
                    target[...] = kernel[place]
                else:
                    target[...] = jnp.zeros((channels, channels), BF16)


def place_both(out, kernel):
    channels = kernel.shape[2]
    for down in range(3):
        for side in range(3):
            begin = (3 * down + side) * channels
            out[begin : begin + channels, :channels] = kernel[down, side]
            out[begin : begin + channels, channels:] = kernel[side, down]


def place_twice(out, matrix):
    channels = matrix.shape[0]
    value = (matrix[...].astype(F32) * 0.5).astype(BF16)
    zero = jnp.zeros((channels, channels), BF16)
    out[:channels, :channels] = value
    out[channels:, channels:] = value
    out[:channels, channels:] = zero
    out[channels:, :channels] = zero


def fill_edges(ext, row_near, row_far, col_near, col_far, size):
    rows = size + 2 * HALO
    tail = LEAD + size + PAD
    ext[:, 0 : LEAD - PAD, :] = jnp.zeros((rows, LEAD - PAD, ext.shape[2]), BF16)
    ext[:, tail:, :] = jnp.zeros((rows, ext.shape[1] - tail, ext.shape[2]), BF16)

    def place(axis, near, far, low, high):
        even = lax.rem(lax.axis_index(axis), 2) == 0

        @pl.when(even)
        def _():
            low[...] = far[...]
            high[...] = near[...]

        @pl.when(jnp.logical_not(even))
        def _():
            low[...] = near[...]
            high[...] = far[...]

    within = slice(LEAD, LEAD + size)
    place(
        "row", row_near, row_far, ext.at[0:HALO, within], ext.at[HALO + size :, within]
    )
    place(
        "col",
        col_near,
        col_far,
        ext.at[:, LEAD - PAD : LEAD],
        ext.at[:, LEAD + size : tail],
    )


def near_block(wide, taps, bias, mix, group, groups, width, channels):
    rows = groups * NEAR * width
    part = jnp.concatenate(
        [
            wide[pl.ds(group + tap // 2, groups), tap % 2].reshape(rows, 3 * channels)
            for tap in range(4)
        ],
        axis=1,
    )
    total = jnp.dot(part, taps[...], preferred_element_type=F32)
    both = jnp.concatenate([bias[...], bias[...]], axis=1)
    active = jnp.maximum(total + both, 0.0).astype(BF16)
    return jnp.dot(active, mix[...], preferred_element_type=F32)


def center_rows(wide, half, group, groups, channels):
    center = wide[pl.ds(group + half, groups), 1 - half]
    return center[..., channels : 2 * channels].astype(F32)


def widen(ext, wide, width, start, channels):
    for tap in range(3):
        begin = start + (tap - 1) * NEAR
        lanes = slice(tap * channels, (tap + 1) * channels)
        for row in range(ext.shape[0]):
            group, rest = divmod(row, 2 * NEAR)
            wide[group, rest // NEAR, rest % NEAR, :, lanes] = ext[
                row, begin : begin + width, :
            ]


def own_kernel(
    tile,
    row_near,
    row_far,
    col_near,
    col_far,
    kernel,
    bias,
    mixer,
    shift,
    far_kernel,
    far_mixer,
    out,
    mirror_taps,
    mix,
    far_taps,
    far_mix,
    ext,
    wide,
    taps,
    *,
    steps,
):
    place_pairs(taps, kernel, False)
    place_pairs(mirror_taps, kernel, True)
    place_twice(mix, mixer)
    place_both(far_taps, far_kernel)
    place_twice(far_mix, far_mixer)
    size, channels = tile.shape[0], tile.shape[2]
    width = size + 2 * PAD
    fill_edges(ext, row_near, row_far, col_near, col_far, size)
    ext[HALO : HALO + size, LEAD : LEAD + size, :] = tile[...]
    widen(ext, wide, width, LEAD - PAD, channels)
    groups = out.shape[0] // steps

    def step(k, carry):
        group = k * groups
        mixed = near_block(wide, taps, bias, mix, group, groups, width, channels)
        for half in range(2):
            part = mixed[:, half * channels : (half + 1) * channels]
            part = part.reshape(groups, NEAR, width, channels)
            value = center_rows(wide, half, group, groups, channels) * 0.5 + part
            out[pl.ds(group, groups), half] = (value + shift[...]).astype(BF16)
        return carry

    lax.fori_loop(0, steps, step, 0)


def place_mirror(ext, frame, inside, size):
    channels = ext.shape[2]
    high = size - 2 * HALO
    band, side = HALO * size, high * PAD
    top, low = 2 * HALO, HALO + size - HALO
    lead, tail = LEAD + PAD, LEAD + size - PAD
    ext[HALO:top, LEAD : LEAD + size, :] = frame[0:band].reshape(HALO, size, channels)
    ext[low : low + HALO, LEAD : LEAD + size, :] = frame[band : 2 * band].reshape(
        HALO, size, channels
    )
    ext[top:low, LEAD:lead, :] = frame[2 * band : 2 * band + side].reshape(
        high, PAD, channels
    )
    ext[top:low, tail : tail + PAD, :] = frame[2 * band + side :].reshape(
        high, PAD, channels
    )
    ext[top:low, lead:tail, :] = inside[...]


def main_kernel(
    frame,
    own,
    direct,
    relayed,
    row_near,
    row_far,
    col_near,
    col_far,
    summed,
    taps,
    bias,
    mix,
    far_taps,
    far_bias,
    far_mix,
    far_shift,
    out,
    ext,
    wide,
    far_wide,
    stage,
    sems,
    *,
    steps,
    far_rows,
):
    size, channels = out.shape[0], out.shape[2]
    width = size + 2 * PAD
    row, col = lax.axis_index("row"), lax.axis_index("col")
    last = lax.axis_size("row") - 1
    diagonal = row == col
    anti = jnp.logical_and(row + col == last, row != col)
    plain = jnp.logical_not(jnp.logical_or(diagonal, anti))

    fill_edges(ext, row_near, row_far, col_near, col_far, size)
    for source, chosen in ((own, diagonal), (direct, plain), (relayed, anti)):

        @pl.when(chosen)
        def _(source=source):
            place_mirror(ext, frame, source, size)

    widen(ext, wide, width, LEAD - PAD, channels)
    groups = summed.shape[0] // steps
    far_groups = far_wide.shape[0]

    def step(k, carry):
        group = k * groups
        mixed = near_block(wide, taps, bias, mix, group, groups, width, channels)
        for half in range(2):
            part = mixed[:, half * channels : (half + 1) * channels]
            part = part.reshape(groups, NEAR, width, channels)
            value = center_rows(wide, half, group, groups, channels) * 0.5 + part
            value = value + summed[pl.ds(group, groups), half].astype(F32)
            value = jnp.maximum(value, 0.0).astype(BF16)
            for tap in range(3):
                begin = PAD + (tap - 1) * FAR
                lanes = slice(tap * channels, (tap + 1) * channels)
                far_wide[pl.ds(group, groups), half, :, :, lanes] = value[
                    :, :, begin : begin + size, :
                ]
        return carry

    lax.fori_loop(0, steps, step, 0)

    edge = FAR // (2 * NEAR)

    @pl.when(row == 0)
    def _():
        far_wide[0:edge] = jnp.zeros((edge,) + far_wide.shape[1:], BF16)

    @pl.when(row == last)
    def _():
        far_wide[far_groups - edge :] = jnp.zeros((edge,) + far_wide.shape[1:], BF16)

    outside = far_wide.shape[:3] + (FAR, channels)

    @pl.when(col == 0)
    def _():
        far_wide[:, :, :, 0:FAR, :channels] = jnp.zeros(outside, BF16)

    @pl.when(col == last)
    def _():
        far_wide[:, :, :, size - FAR :, 2 * channels :] = jnp.zeros(outside, BF16)

    def copy(slot, base):
        return pltpu.make_async_copy(
            stage.at[slot], out.at[pl.ds(base, far_rows)], sems.at[slot]
        )

    count = size // far_rows

    def far_step(k, carry):
        slot = lax.rem(k, 2)
        base = k * (far_rows // FAR)

        @pl.when(k >= 2)
        def _():
            copy(slot, (k - 2) * far_rows).wait()

        rows = far_rows * size
        part = jnp.concatenate(
            [
                far_wide[pl.ds(base + tap, far_rows // FAR)].reshape(rows, 3 * channels)
                for tap in range(3)
            ],
            axis=1,
        )
        total = jnp.dot(part, far_taps[...], preferred_element_type=F32)
        active = jnp.maximum(total[:, :channels] + far_bias[...], 0.0)
        active = active + jnp.maximum(total[:, channels:] + far_bias[...], 0.0)
        active = active.astype(BF16)
        active = jnp.concatenate([active[: rows // 2], active[rows // 2 :]], axis=1)
        mixed = jnp.dot(active, far_mix[...], preferred_element_type=F32)
        mixed = jnp.concatenate([mixed[:, :channels], mixed[:, channels:]], axis=0)
        center = far_wide[
            pl.ds(base + 1, far_rows // FAR), :, :, :, channels : 2 * channels
        ]
        center = center.reshape(rows, channels).astype(F32)
        value = jnp.maximum(center + far_shift[...] + mixed, 0.0)
        stage[slot] = value.reshape(far_rows, size, channels)
        copy(slot, k * far_rows).start()
        return carry

    lax.fori_loop(0, count, far_step, 0)
    for k in range(max(count - 2, 0), count):
        copy(k % 2, k * far_rows).wait()


def edge_strips(frame, size):
    high = size - 2 * HALO
    channels = frame.shape[1]
    band, side = HALO * size, high * PAD
    top = frame[0:band].reshape(HALO, size, channels)
    low = frame[band : 2 * band].reshape(HALO, size, channels)
    left = frame[2 * band : 2 * band + side].reshape(high, PAD, channels)
    right = frame[2 * band + side :].reshape(high, PAD, channels)
    left = jnp.concatenate([top[:, :PAD], left, low[:, :PAD]], axis=0)
    right = jnp.concatenate([top[:, size - PAD :], right, low[:, size - PAD :]], axis=0)
    return top, low, left, right


def exchange(low, high, axis):
    count = lax.axis_size(axis)
    even = lax.axis_index(axis) % 2 == 0

    def swap(first, value):
        pairs = [(i, i + 1) for i in range(first, count - 1, 2)]
        return lax.ppermute(value, axis, pairs + [(j, i) for i, j in pairs])

    near = swap(0, jnp.where(even, high, low))
    far = swap(1, jnp.where(even, low, high))
    return near, far


def halo_pieces(top, low, left, right):
    size = top.shape[1]
    near, far = exchange(top, low, "row")
    even = lax.axis_index("row") % 2 == 0
    above, below = jnp.where(even, far, near), jnp.where(even, near, far)
    start = jnp.concatenate([above[:, :PAD], left, below[:, :PAD]], axis=0)
    end = jnp.concatenate(
        [above[:, size - PAD :], right, below[:, size - PAD :]], axis=0
    )
    return (near, far) + exchange(start, end, "col")


def compute(
    features,
    kernel_first,
    bias_first,
    mixer_first,
    shift_first,
    kernel_second,
    bias_second,
    mixer_second,
    shift_second,
):
    size, _, channels = features.shape
    count = lax.axis_size("row")
    rows = size + 2 * HALO
    width = size + 2 * PAD
    groups = (size + 2 * FAR) // (2 * NEAR)
    pair = ("row", "col")
    straight, hop, onward = mirror_routes(count)

    def send(value, route):
        return lax.ppermute(value, pair, route)

    turn = lambda part: jnp.swapaxes(part, 0, 1)
    frame = jnp.concatenate(
        [
            turn(piece).reshape(-1, channels)
            for piece in (
                features[:, :HALO],
                features[:, size - HALO :],
                features[:PAD, HALO : size - HALO],
                features[size - PAD :, HALO : size - HALO],
            )
        ],
        axis=0,
    )
    inside = turn(features[PAD : size - PAD, HALO : size - HALO])
    direct_frame = send(frame, straight + hop)
    hop_inside = send(inside, hop)
    direct = send(inside, straight)
    relayed_frame = send(direct_frame, onward)
    relayed = send(hop_inside, onward)

    row, col = lax.axis_index("row"), lax.axis_index("col")
    diagonal = row == col
    anti = row + col == count - 1
    mirror_frame = jnp.where(
        diagonal, frame, jnp.where(anti, relayed_frame, direct_frame)
    )
    own_halos = halo_pieces(
        features[:HALO],
        features[size - HALO :],
        features[:, :PAD],
        features[:, size - PAD :],
    )
    halos = halo_pieces(*edge_strips(mirror_frame, size))

    whole = pl.BlockSpec(memory_space=pltpu.VMEM)
    line = lambda v: v.reshape(1, channels)
    ext = pltpu.VMEM((rows, 2 * LEAD + size, channels), BF16)
    wide = pltpu.VMEM(
        (rows // (2 * NEAR), 2, NEAR, width, 3 * channels), BF16
    )
    field = (groups, 2, NEAR, width, channels)
    pairs = (12 * channels, 2 * channels)
    square = (2 * channels, 2 * channels)
    near_flops = 2 * groups * 2 * NEAR * width * 10 * channels * channels
    own_block = pl.pallas_call(
        functools.partial(own_kernel, steps=1),
        out_shape=[
            jax.ShapeDtypeStruct(shape, BF16)
            for shape in (field, pairs, square, (9 * channels, 2 * channels), square)
        ],
        in_specs=[whole] * 11,
        out_specs=[whole] * 5,
        scratch_shapes=[ext, wide, pltpu.VMEM(pairs, BF16)],
        cost_estimate=pl.CostEstimate(
            flops=2 * near_flops, bytes_accessed=8 << 20, transcendentals=0
        ),
        compiler_params=pltpu.CompilerParams(vmem_limit_bytes=GRANT),
        name="own_block",
    )
    own_operands = (
        features,
        *own_halos,
        kernel_first,
        line(bias_first),
        mixer_first,
        line(shift_first),
        kernel_second,
        mixer_second,
    )
    summed, taps, mix, far_taps, far_mix = own_block(*own_operands)

    far_rows = size // 2
    return pl.pallas_call(
        functools.partial(main_kernel, steps=1, far_rows=far_rows),
        out_shape=jax.ShapeDtypeStruct(features.shape, F32),
        in_specs=[whole] * 16,
        out_specs=pl.BlockSpec(memory_space=pl.ANY),
        scratch_shapes=[
            ext,
            wide,
            pltpu.VMEM((groups, 2, NEAR, size, 3 * channels), BF16),
            pltpu.VMEM((2, far_rows, size, channels), F32),
            pltpu.SemaphoreType.DMA((2,)),
        ],
        cost_estimate=pl.CostEstimate(
            flops=4 * near_flops, bytes_accessed=16 << 20, transcendentals=0
        ),
        compiler_params=pltpu.CompilerParams(vmem_limit_bytes=GRANT),
        name="main_block",
    )(
        mirror_frame,
        inside,
        direct,
        relayed,
        *halos,
        summed,
        taps,
        line(bias_first),
        mix,
        far_taps,
        line(bias_second),
        far_mix,
        line(shift_second),
    )


def solution(mesh):
    return jax.shard_map(
        compute,
        mesh=mesh,
        in_specs=(P(("groups", "row"), "col", None), P(), P(), P(), P(), P(), P(), P(), P()),
        out_specs=P(("groups", "row"), "col", None),
        check_vma=False,
    )
```

```python
import functools

import jax
import jax.numpy as jnp
from jax import lax
from jax.experimental import pallas as pl
from jax.experimental.pallas import tpu as pltpu
from jax.sharding import PartitionSpec as P


BF16 = jnp.bfloat16
F32 = jnp.float32
NEAR = 2
FAR = 4
HALO = NEAR + FAR
PAD = 8
LEAD = 16
GRANT = 28 << 20


def mirror_routes(count):
    straight, hop, onward = [], [], []
    for r in range(count):
        for c in range(count):
            if r == c:
                continue
            if r + c == count - 1:
                hop.append((r * count + c, c * count + c))
                onward.append((c * count + c, c * count + r))
            else:
                straight.append((r * count + c, c * count + r))
    return straight, hop, onward


def place_pairs(out, kernel, turned):
    channels = kernel.shape[2]
    for tap in range(4):
        for half in range(2):
            for side in range(3):
                begin = (3 * tap + side) * channels
                target = out.at[
                    begin : begin + channels, half * channels : (half + 1) * channels
                ]
                down = tap - half
                if 0 <= down < 3:
                    place = (side, down) if turned else (down, side)
                    target[...] = kernel[place]
                else:
                    target[...] = jnp.zeros((channels, channels), BF16)


def place_both(out, kernel):
    channels = kernel.shape[2]
    for down in range(3):
        for side in range(3):
            begin = (3 * down + side) * channels
            out[begin : begin + channels, :channels] = kernel[down, side]
            out[begin : begin + channels, channels:] = kernel[side, down]


def place_twice(out, matrix):
    channels = matrix.shape[0]
    value = (matrix[...].astype(F32) * 0.5).astype(BF16)
    zero = jnp.zeros((channels, channels), BF16)
    out[:channels, :channels] = value
    out[channels:, channels:] = value
    out[:channels, channels:] = zero
    out[channels:, :channels] = zero


def fill_edges(ext, row_near, row_far, col_near, col_far, spread, dense, size):
    rows = size + 2 * HALO
    channels = ext.shape[2]
    tail = LEAD + size + PAD
    within = slice(LEAD, LEAD + size)
    even_row = lax.rem(lax.axis_index("row"), 2) == 0
    even_col = lax.rem(lax.axis_index("col"), 2) == 0
    ext[:, 0 : LEAD - PAD, :] = jnp.zeros((rows, LEAD - PAD, channels), BF16)
    ext[:, tail:, :] = jnp.zeros((rows, ext.shape[1] - tail, channels), BF16)

    for even, above, below in ((True, row_far, row_near), (False, row_near, row_far)):

        @pl.when(even_row if even else jnp.logical_not(even_row))
        def _(above=above, below=below):
            ext[0:HALO, within, :] = above[...]
            ext[HALO + size :, within, :] = below[...]

    for side in range(2):

        @pl.when(even_col)
        def _(side=side):
            dense[...] = (col_near if side else col_far)[...].astype(F32)

        @pl.when(jnp.logical_not(even_col))
        def _(side=side):
            dense[...] = (col_far if side else col_near)[...].astype(F32)

        for c in range(PAD):
            line = c - (PAD - HALO) * (1 - side)
            if 0 <= line < HALO:
                value = dense[line * rows : (line + 1) * rows, :]
            else:
                value = jnp.zeros((rows, channels), F32)
            spread[pl.ds(c, rows, stride=PAD), :] = value
        begin = LEAD + size if side else LEAD - PAD
        ext[:, begin : begin + PAD, :] = (
            spread[...].reshape(rows, PAD, channels).astype(BF16)
        )


def near_block(wide, taps, bias, mix, group, groups, width, channels):
    rows = groups * NEAR * width
    part = jnp.concatenate(
        [
            wide[pl.ds(group + tap // 2, groups), tap % 2].reshape(rows, 3 * channels)
            for tap in range(4)
        ],
        axis=1,
    )
    total = jnp.dot(part, taps[...], preferred_element_type=F32)
    both = jnp.concatenate([bias[...], bias[...]], axis=1)
    active = jnp.maximum(total + both, 0.0).astype(BF16)
    return jnp.dot(active, mix[...], preferred_element_type=F32)


def center_rows(wide, half, group, groups, channels):
    center = wide[pl.ds(group + half, groups), 1 - half]
    return center[..., channels : 2 * channels].astype(F32)


def widen(ext, wide, width, start, channels):
    for tap in range(3):
        begin = start + (tap - 1) * NEAR
        lanes = slice(tap * channels, (tap + 1) * channels)
        for row in range(ext.shape[0]):
            group, rest = divmod(row, 2 * NEAR)
            wide[group, rest // NEAR, rest % NEAR, :, lanes] = ext[
                row, begin : begin + width, :
            ]


def own_kernel(
    tile,
    row_near,
    row_far,
    col_near,
    col_far,
    kernel,
    bias,
    mixer,
    shift,
    far_kernel,
    far_mixer,
    out,
    mirror_taps,
    mix,
    far_taps,
    far_mix,
    ext,
    wide,
    taps,
    spread,
    dense,
    *,
    steps,
):
    place_pairs(taps, kernel, False)
    place_pairs(mirror_taps, kernel, True)
    place_twice(mix, mixer)
    place_both(far_taps, far_kernel)
    place_twice(far_mix, far_mixer)
    size, channels = tile.shape[0], tile.shape[2]
    width = size + 2 * PAD
    fill_edges(ext, row_near, row_far, col_near, col_far, spread, dense, size)
    ext[HALO : HALO + size, LEAD : LEAD + size, :] = tile[...]
    widen(ext, wide, width, LEAD - PAD, channels)
    groups = out.shape[0] // steps

    def step(k, carry):
        group = k * groups
        mixed = near_block(wide, taps, bias, mix, group, groups, width, channels)
        for half in range(2):
            part = mixed[:, half * channels : (half + 1) * channels]
            part = part.reshape(groups, NEAR, width, channels)
            value = center_rows(wide, half, group, groups, channels) * 0.5 + part
            out[pl.ds(group, groups), half] = (value + shift[...]).astype(BF16)
        return carry

    lax.fori_loop(0, steps, step, 0)


def place_mirror(ext, frame, inside, size):
    channels = ext.shape[2]
    high = size - 2 * HALO
    band, side = HALO * size, high * PAD
    top, low = 2 * HALO, HALO + size - HALO
    lead, tail = LEAD + PAD, LEAD + size - PAD
    ext[HALO:top, LEAD : LEAD + size, :] = frame[0:band].reshape(HALO, size, channels)
    ext[low : low + HALO, LEAD : LEAD + size, :] = frame[band : 2 * band].reshape(
        HALO, size, channels
    )
    ext[top:low, LEAD:lead, :] = frame[2 * band : 2 * band + side].reshape(
        high, PAD, channels
    )
    ext[top:low, tail : tail + PAD, :] = frame[2 * band + side :].reshape(
        high, PAD, channels
    )
    ext[top:low, lead:tail, :] = inside[...]


def main_kernel(
    frame,
    own,
    direct,
    relayed,
    row_near,
    row_far,
    col_near,
    col_far,
    summed,
    taps,
    bias,
    mix,
    far_taps,
    far_bias,
    far_mix,
    far_shift,
    out,
    ext,
    wide,
    far_wide,
    stage,
    sems,
    spread,
    dense,
    *,
    steps,
    far_rows,
):
    size, channels = out.shape[0], out.shape[2]
    width = size + 2 * PAD
    row, col = lax.axis_index("row"), lax.axis_index("col")
    last = lax.axis_size("row") - 1
    diagonal = row == col
    anti = jnp.logical_and(row + col == last, row != col)
    plain = jnp.logical_not(jnp.logical_or(diagonal, anti))

    fill_edges(ext, row_near, row_far, col_near, col_far, spread, dense, size)
    for source, chosen in ((own, diagonal), (direct, plain), (relayed, anti)):

        @pl.when(chosen)
        def _(source=source):
            place_mirror(ext, frame, source, size)

    widen(ext, wide, width, LEAD - PAD, channels)
    groups = summed.shape[0] // steps
    far_groups = far_wide.shape[0]

    def step(k, carry):
        group = k * groups
        mixed = near_block(wide, taps, bias, mix, group, groups, width, channels)
        for half in range(2):
            part = mixed[:, half * channels : (half + 1) * channels]
            part = part.reshape(groups, NEAR, width, channels)
            value = center_rows(wide, half, group, groups, channels) * 0.5 + part
            value = value + summed[pl.ds(group, groups), half].astype(F32)
            value = jnp.maximum(value, 0.0).astype(BF16)
            for tap in range(3):
                begin = PAD + (tap - 1) * FAR
                lanes = slice(tap * channels, (tap + 1) * channels)
                far_wide[pl.ds(group, groups), half, :, :, lanes] = value[
                    :, :, begin : begin + size, :
                ]
        return carry

    lax.fori_loop(0, steps, step, 0)

    edge = FAR // (2 * NEAR)

    @pl.when(row == 0)
    def _():
        far_wide[0:edge] = jnp.zeros((edge,) + far_wide.shape[1:], BF16)

    @pl.when(row == last)
    def _():
        far_wide[far_groups - edge :] = jnp.zeros((edge,) + far_wide.shape[1:], BF16)

    outside = far_wide.shape[:3] + (FAR, channels)

    @pl.when(col == 0)
    def _():
        far_wide[:, :, :, 0:FAR, :channels] = jnp.zeros(outside, BF16)

    @pl.when(col == last)
    def _():
        far_wide[:, :, :, size - FAR :, 2 * channels :] = jnp.zeros(outside, BF16)

    def copy(slot, base):
        return pltpu.make_async_copy(
            stage.at[slot], out.at[pl.ds(base, far_rows)], sems.at[slot]
        )

    count = size // far_rows

    def far_step(k, carry):
        slot = lax.rem(k, 2)
        base = k * (far_rows // FAR)

        @pl.when(k >= 2)
        def _():
            copy(slot, (k - 2) * far_rows).wait()

        rows = far_rows * size
        part = jnp.concatenate(
            [
                far_wide[pl.ds(base + tap, far_rows // FAR)].reshape(rows, 3 * channels)
                for tap in range(3)
            ],
            axis=1,
        )
        total = jnp.dot(part, far_taps[...], preferred_element_type=F32)
        active = jnp.maximum(total[:, :channels] + far_bias[...], 0.0)
        active = active + jnp.maximum(total[:, channels:] + far_bias[...], 0.0)
        active = active.astype(BF16)
        active = jnp.concatenate([active[: rows // 2], active[rows // 2 :]], axis=1)
        mixed = jnp.dot(active, far_mix[...], preferred_element_type=F32)
        mixed = jnp.concatenate([mixed[:, :channels], mixed[:, channels:]], axis=0)
        center = far_wide[
            pl.ds(base + 1, far_rows // FAR), :, :, :, channels : 2 * channels
        ]
        center = center.reshape(rows, channels).astype(F32)
        value = jnp.maximum(center + far_shift[...] + mixed, 0.0)
        stage[slot] = value.reshape(far_rows, size, channels)
        copy(slot, k * far_rows).start()
        return carry

    lax.fori_loop(0, count, far_step, 0)
    for k in range(max(count - 2, 0), count):
        copy(k % 2, k * far_rows).wait()


def edge_strips(frame, size):
    high = size - 2 * HALO
    channels = frame.shape[1]
    band, side = HALO * size, high * PAD
    top = frame[0:band].reshape(HALO, size, channels)
    low = frame[band : 2 * band].reshape(HALO, size, channels)
    left = frame[2 * band : 2 * band + side].reshape(high, PAD, channels)
    right = frame[2 * band + side :].reshape(high, PAD, channels)
    left = jnp.concatenate([top[:, :PAD], left, low[:, :PAD]], axis=0)
    right = jnp.concatenate([top[:, size - PAD :], right, low[:, size - PAD :]], axis=0)
    return top, low, left, right


def swap_pairs(near, far, axis):
    count = lax.axis_size(axis)

    def swap(first, value):
        pairs = [(i, i + 1) for i in range(first, count - 1, 2)]
        return lax.ppermute(value, axis, pairs + [(j, i) for i, j in pairs])

    near = swap(0, near)
    far = swap(1, far)
    return near, far


def exchange(low, high, axis):
    even = lax.axis_index(axis) % 2 == 0
    return swap_pairs(jnp.where(even, high, low), jnp.where(even, low, high), axis)


def strip_kernel(left, right, row_near, row_far, near, far, wide, dense):
    size, _, channels = left.shape
    width = row_near.shape[1]
    rows = size + 2 * HALO
    head = HALO * PAD
    even_row = lax.rem(lax.axis_index("row"), 2) == 0
    even_col = lax.rem(lax.axis_index("col"), 2) == 0

    for side, edge in enumerate((left, right)):
        columns = slice(side * (width - PAD), side * (width - PAD) + PAD)
        wide[head : head + size * PAD, :] = (
            edge[...].reshape(size * PAD, channels).astype(F32)
        )
        for even, above, below in (
            (True, row_far, row_near),
            (False, row_near, row_far),
        ):

            @pl.when(even_row if even else jnp.logical_not(even_row))
            def _(above=above, below=below, columns=columns):
                wide[0:head, :] = (
                    above[:, columns, :].reshape(head, channels).astype(F32)
                )
                wide[head + size * PAD :, :] = (
                    below[:, columns, :].reshape(head, channels).astype(F32)
                )

        for c in range(HALO):
            line = c + side * (PAD - HALO)
            dense[c * rows : (c + 1) * rows, :] = wide[pl.ds(line, rows, stride=PAD), :]

        packed = dense[...].astype(BF16)

        @pl.when(even_col)
        def _(side=side, packed=packed):
            (near if side else far)[...] = packed

        @pl.when(jnp.logical_not(even_col))
        def _(side=side, packed=packed):
            (far if side else near)[...] = packed


def halo_pieces(top, low, left, right):
    size, channels = left.shape[0], left.shape[2]
    rows = size + 2 * HALO
    row_near, row_far = exchange(top, low, "row")
    whole = pl.BlockSpec(memory_space=pltpu.VMEM)
    strip = jax.ShapeDtypeStruct((HALO * rows, channels), BF16)
    near, far = pl.pallas_call(
        strip_kernel,
        out_shape=[strip, strip],
        in_specs=[whole] * 4,
        out_specs=[whole] * 2,
        scratch_shapes=[
            pltpu.VMEM((PAD * rows, channels), F32),
            pltpu.VMEM((HALO * rows, channels), F32),
        ],
        compiler_params=pltpu.CompilerParams(vmem_limit_bytes=GRANT // 4),
    )(left, right, row_near, row_far)
    return (row_near, row_far) + swap_pairs(near, far, "col")


def compute(
    features,
    kernel_first,
    bias_first,
    mixer_first,
    shift_first,
    kernel_second,
    bias_second,
    mixer_second,
    shift_second,
):
    size, _, channels = features.shape
    count = lax.axis_size("row")
    rows = size + 2 * HALO
    width = size + 2 * PAD
    groups = (size + 2 * FAR) // (2 * NEAR)
    pair = ("row", "col")
    straight, hop, onward = mirror_routes(count)

    def send(value, route):
        return lax.ppermute(value, pair, route)

    turn = lambda part: jnp.swapaxes(part, 0, 1)
    frame = jnp.concatenate(
        [
            turn(piece).reshape(-1, channels)
            for piece in (
                features[:, :HALO],
                features[:, size - HALO :],
                features[:PAD, HALO : size - HALO],
                features[size - PAD :, HALO : size - HALO],
            )
        ],
        axis=0,
    )
    inside = turn(features[PAD : size - PAD, HALO : size - HALO])
    direct_frame = send(frame, straight + hop)
    hop_inside = send(inside, hop)
    direct = send(inside, straight)
    relayed_frame = send(direct_frame, onward)
    relayed = send(hop_inside, onward)

    row, col = lax.axis_index("row"), lax.axis_index("col")
    diagonal = row == col
    anti = row + col == count - 1
    mirror_frame = jnp.where(
        diagonal, frame, jnp.where(anti, relayed_frame, direct_frame)
    )
    own_halos = halo_pieces(
        features[:HALO],
        features[size - HALO :],
        features[:, :PAD],
        features[:, size - PAD :],
    )
    halos = halo_pieces(*edge_strips(mirror_frame, size))

    whole = pl.BlockSpec(memory_space=pltpu.VMEM)
    line = lambda v: v.reshape(1, channels)
    ext = pltpu.VMEM((rows, 2 * LEAD + size, channels), BF16)
    wide = pltpu.VMEM(
        (rows // (2 * NEAR), 2, NEAR, width, 3 * channels), BF16
    )
    lines = [
        pltpu.VMEM((PAD * rows, channels), F32),
        pltpu.VMEM((HALO * rows, channels), F32),
    ]
    field = (groups, 2, NEAR, width, channels)
    pairs = (12 * channels, 2 * channels)
    square = (2 * channels, 2 * channels)
    near_flops = 2 * groups * 2 * NEAR * width * 10 * channels * channels
    own_block = pl.pallas_call(
        functools.partial(own_kernel, steps=1),
        out_shape=[
            jax.ShapeDtypeStruct(shape, BF16)
            for shape in (field, pairs, square, (9 * channels, 2 * channels), square)
        ],
        in_specs=[whole] * 11,
        out_specs=[whole] * 5,
        scratch_shapes=[ext, wide, pltpu.VMEM(pairs, BF16)] + lines,
        cost_estimate=pl.CostEstimate(
            flops=2 * near_flops, bytes_accessed=8 << 20, transcendentals=0
        ),
        compiler_params=pltpu.CompilerParams(vmem_limit_bytes=GRANT),
        name="own_block",
    )
    own_operands = (
        features,
        *own_halos,
        kernel_first,
        line(bias_first),
        mixer_first,
        line(shift_first),
        kernel_second,
        mixer_second,
    )
    summed, taps, mix, far_taps, far_mix = own_block(*own_operands)

    far_rows = size // 2
    return pl.pallas_call(
        functools.partial(main_kernel, steps=1, far_rows=far_rows),
        out_shape=jax.ShapeDtypeStruct(features.shape, F32),
        in_specs=[whole] * 16,
        out_specs=pl.BlockSpec(memory_space=pl.ANY),
        scratch_shapes=[
            ext,
            wide,
            pltpu.VMEM((groups, 2, NEAR, size, 3 * channels), BF16),
            pltpu.VMEM((2, far_rows, size, channels), F32),
            pltpu.SemaphoreType.DMA((2,)),
        ]
        + lines,
        cost_estimate=pl.CostEstimate(
            flops=4 * near_flops, bytes_accessed=16 << 20, transcendentals=0
        ),
        compiler_params=pltpu.CompilerParams(vmem_limit_bytes=GRANT),
        name="main_block",
    )(
        mirror_frame,
        inside,
        direct,
        relayed,
        *halos,
        summed,
        taps,
        line(bias_first),
        mix,
        far_taps,
        line(bias_second),
        far_mix,
        line(shift_second),
    )


def solution(mesh):
    return jax.shard_map(
        compute,
        mesh=mesh,
        in_specs=(P(("groups", "row"), "col", None), P(), P(), P(), P(), P(), P(), P(), P()),
        out_specs=P(("groups", "row"), "col", None),
        check_vma=False,
    )
```

```python
import functools

import jax
import jax.numpy as jnp
from jax import lax
from jax.experimental import pallas as pl
from jax.experimental.pallas import tpu as pltpu
from jax.sharding import PartitionSpec as P


BF16 = jnp.bfloat16
F32 = jnp.float32
NEAR = 2
FAR = 4
HALO = NEAR + FAR
PAD = 8
LEAD = 16
GRANT = 28 << 20


def mirror_routes(count):
    straight, hop, onward = [], [], []
    for r in range(count):
        for c in range(count):
            if r == c:
                continue
            if r + c == count - 1:
                hop.append((r * count + c, c * count + c))
                onward.append((c * count + c, c * count + r))
            else:
                straight.append((r * count + c, c * count + r))
    return straight, hop, onward


def place_pairs(out, kernel, turned):
    channels = kernel.shape[2]
    for tap in range(4):
        for half in range(2):
            for side in range(3):
                begin = (3 * tap + side) * channels
                target = out.at[
                    begin : begin + channels, half * channels : (half + 1) * channels
                ]
                down = tap - half
                if 0 <= down < 3:
                    place = (side, down) if turned else (down, side)
                    target[...] = kernel[place]
                else:
                    target[...] = jnp.zeros((channels, channels), BF16)


def place_both(out, kernel):
    channels = kernel.shape[2]
    begin = 0
    for down in range(3):
        for side in range(3):
            if down != side:
                out[begin : begin + channels, :channels] = kernel[down, side]
                out[begin : begin + channels, channels:] = kernel[side, down]
                begin += channels
    zero = jnp.zeros((channels, channels), BF16)
    for half in range(2):
        for down in range(3):
            for other in range(2):
                out[
                    begin : begin + channels,
                    other * channels : (other + 1) * channels,
                ] = kernel[down, down] if other == half else zero
            begin += channels


def place_twice(out, matrix):
    channels = matrix.shape[0]
    value = (matrix[...].astype(F32) * 0.5).astype(BF16)
    zero = jnp.zeros((channels, channels), BF16)
    out[:channels, :channels] = value
    out[channels:, channels:] = value
    out[:channels, channels:] = zero
    out[channels:, :channels] = zero


def fill_edges(ext, row_near, row_far, col_near, col_far, spread, dense, size):
    rows = size + 2 * HALO
    channels = ext.shape[2]
    tail = LEAD + size + PAD
    within = slice(LEAD, LEAD + size)
    even_row = lax.rem(lax.axis_index("row"), 2) == 0
    even_col = lax.rem(lax.axis_index("col"), 2) == 0
    ext[:, 0 : LEAD - PAD, :] = jnp.zeros((rows, LEAD - PAD, channels), BF16)
    ext[:, tail:, :] = jnp.zeros((rows, ext.shape[1] - tail, channels), BF16)

    for even, above, below in ((True, row_far, row_near), (False, row_near, row_far)):

        @pl.when(even_row if even else jnp.logical_not(even_row))
        def _(above=above, below=below):
            ext[0:HALO, within, :] = above[...]
            ext[HALO + size :, within, :] = below[...]

    for side in range(2):

        @pl.when(even_col)
        def _(side=side):
            dense[...] = (col_near if side else col_far)[...].astype(F32)

        @pl.when(jnp.logical_not(even_col))
        def _(side=side):
            dense[...] = (col_far if side else col_near)[...].astype(F32)

        for c in range(PAD):
            line = c - (PAD - HALO) * (1 - side)
            if 0 <= line < HALO:
                value = dense[line * rows : (line + 1) * rows, :]
            else:
                value = jnp.zeros((rows, channels), F32)
            spread[pl.ds(c, rows, stride=PAD), :] = value
        begin = LEAD + size if side else LEAD - PAD
        ext[:, begin : begin + PAD, :] = (
            spread[...].reshape(rows, PAD, channels).astype(BF16)
        )


def near_block(wide, taps, bias, mix, group, groups, width, channels):
    rows = groups * NEAR * width
    part = jnp.concatenate(
        [
            wide[pl.ds(group + tap // 2, groups), tap % 2].reshape(rows, 3 * channels)
            for tap in range(4)
        ],
        axis=1,
    )
    total = jnp.dot(part, taps[...], preferred_element_type=F32)
    both = jnp.concatenate([bias[...], bias[...]], axis=1)
    active = jnp.maximum(total + both, 0.0).astype(BF16)
    return jnp.dot(active, mix[...], preferred_element_type=F32)


def center_rows(wide, half, group, groups, channels):
    center = wide[pl.ds(group + half, groups), 1 - half]
    return center[..., channels : 2 * channels].astype(F32)


def widen(ext, wide, width, start, channels):
    for tap in range(3):
        begin = start + (tap - 1) * NEAR
        lanes = slice(tap * channels, (tap + 1) * channels)
        for row in range(ext.shape[0]):
            group, rest = divmod(row, 2 * NEAR)
            wide[group, rest // NEAR, rest % NEAR, :, lanes] = ext[
                row, begin : begin + width, :
            ]


def own_kernel(
    tile,
    row_near,
    row_far,
    col_near,
    col_far,
    kernel,
    bias,
    mixer,
    shift,
    far_kernel,
    far_mixer,
    out,
    mirror_taps,
    mix,
    far_taps,
    far_mix,
    ext,
    wide,
    taps,
    spread,
    dense,
    *,
    steps,
):
    place_pairs(taps, kernel, False)
    place_pairs(mirror_taps, kernel, True)
    place_twice(mix, mixer)
    place_both(far_taps, far_kernel)
    place_twice(far_mix, far_mixer)
    size, channels = tile.shape[0], tile.shape[2]
    width = size + 2 * PAD
    fill_edges(ext, row_near, row_far, col_near, col_far, spread, dense, size)
    ext[HALO : HALO + size, LEAD : LEAD + size, :] = tile[...]
    widen(ext, wide, width, LEAD - PAD, channels)
    groups = out.shape[0] // steps

    def step(k, carry):
        group = k * groups
        mixed = near_block(wide, taps, bias, mix, group, groups, width, channels)
        for half in range(2):
            part = mixed[:, half * channels : (half + 1) * channels]
            part = part.reshape(groups, NEAR, width, channels)
            value = center_rows(wide, half, group, groups, channels) * 0.5 + part
            out[pl.ds(group, groups), half] = (value + shift[...]).astype(BF16)
        return carry

    lax.fori_loop(0, steps, step, 0)


def place_mirror(ext, frame, inside, size):
    channels = ext.shape[2]
    high = size - 2 * HALO
    band, side = HALO * size, high * PAD
    top, low = 2 * HALO, HALO + size - HALO
    lead, tail = LEAD + PAD, LEAD + size - PAD
    ext[HALO:top, LEAD : LEAD + size, :] = frame[0:band].reshape(HALO, size, channels)
    ext[low : low + HALO, LEAD : LEAD + size, :] = frame[band : 2 * band].reshape(
        HALO, size, channels
    )
    ext[top:low, LEAD:lead, :] = frame[2 * band : 2 * band + side].reshape(
        high, PAD, channels
    )
    ext[top:low, tail : tail + PAD, :] = frame[2 * band + side :].reshape(
        high, PAD, channels
    )
    ext[top:low, lead:tail, :] = inside[...]


def main_kernel(
    frame,
    own,
    direct,
    relayed,
    row_near,
    row_far,
    col_near,
    col_far,
    summed,
    taps,
    bias,
    mix,
    far_taps,
    far_bias,
    far_mix,
    far_shift,
    out,
    ext,
    wide,
    far_wide,
    stage,
    sems,
    spread,
    dense,
    *,
    steps,
    far_rows,
):
    size, channels = out.shape[0], out.shape[2]
    width = size + 2 * PAD
    row, col = lax.axis_index("row"), lax.axis_index("col")
    last = lax.axis_size("row") - 1
    diagonal = row == col
    anti = jnp.logical_and(row + col == last, row != col)
    plain = jnp.logical_not(jnp.logical_or(diagonal, anti))

    fill_edges(ext, row_near, row_far, col_near, col_far, spread, dense, size)
    for source, chosen in ((own, diagonal), (direct, plain), (relayed, anti)):

        @pl.when(chosen)
        def _(source=source):
            place_mirror(ext, frame, source, size)

    widen(ext, wide, width, LEAD - PAD, channels)
    groups = summed.shape[0] // steps
    far_groups = far_wide.shape[0]

    def step(k, carry):
        group = k * groups
        mixed = near_block(wide, taps, bias, mix, group, groups, width, channels)
        for half in range(2):
            part = mixed[:, half * channels : (half + 1) * channels]
            part = part.reshape(groups, NEAR, width, channels)
            value = center_rows(wide, half, group, groups, channels) * 0.5 + part
            value = value + summed[pl.ds(group, groups), half].astype(F32)
            value = jnp.maximum(value, 0.0).astype(BF16)
            for tap in range(3):
                begin = PAD + (tap - 1) * FAR
                lanes = slice(tap * channels, (tap + 1) * channels)
                far_wide[pl.ds(group, groups), half, :, :, lanes] = value[
                    :, :, begin : begin + size, :
                ]
        return carry

    lax.fori_loop(0, steps, step, 0)

    edge = FAR // (2 * NEAR)

    @pl.when(row == 0)
    def _():
        far_wide[0:edge] = jnp.zeros((edge,) + far_wide.shape[1:], BF16)

    @pl.when(row == last)
    def _():
        far_wide[far_groups - edge :] = jnp.zeros((edge,) + far_wide.shape[1:], BF16)

    outside = far_wide.shape[:3] + (FAR, channels)

    @pl.when(col == 0)
    def _():
        far_wide[:, :, :, 0:FAR, :channels] = jnp.zeros(outside, BF16)

    @pl.when(col == last)
    def _():
        far_wide[:, :, :, size - FAR :, 2 * channels :] = jnp.zeros(outside, BF16)

    def copy(slot, base):
        return pltpu.make_async_copy(
            stage.at[slot], out.at[pl.ds(base, far_rows)], sems.at[slot]
        )

    count = size // far_rows

    def far_step(k, carry):
        slot = lax.rem(k, 2)
        base = k * (far_rows // FAR)

        @pl.when(k >= 2)
        def _():
            copy(slot, (k - 2) * far_rows).wait()

        rows = far_rows * size
        views = [
            far_wide[pl.ds(base + tap, far_rows // FAR)].reshape(rows, 3 * channels)
            for tap in range(3)
        ]

        def pick(tap, side):
            return views[tap][:, side * channels : (side + 1) * channels]

        cross = jnp.concatenate(
            [pick(a, b) for a in range(3) for b in range(3) if a != b], axis=1
        )
        total = jnp.dot(
            cross, far_taps[: 6 * channels, :], preferred_element_type=F32
        )
        middle = rows // 2
        line = jnp.concatenate(
            [pick(a, a)[:middle] for a in range(3)]
            + [pick(a, a)[middle:] for a in range(3)],
            axis=1,
        )
        shared = jnp.dot(
            line, far_taps[6 * channels :, :], preferred_element_type=F32
        )
        shared = jnp.concatenate([shared[:, :channels], shared[:, channels:]], axis=0)
        shared = shared + far_bias[...]
        active = jnp.maximum(total[:, :channels] + shared, 0.0)
        active = active + jnp.maximum(total[:, channels:] + shared, 0.0)
        active = active.astype(BF16)
        active = jnp.concatenate([active[: rows // 2], active[rows // 2 :]], axis=1)
        mixed = jnp.dot(active, far_mix[...], preferred_element_type=F32)
        mixed = jnp.concatenate([mixed[:, :channels], mixed[:, channels:]], axis=0)
        center = far_wide[
            pl.ds(base + 1, far_rows // FAR), :, :, :, channels : 2 * channels
        ]
        center = center.reshape(rows, channels).astype(F32)
        value = jnp.maximum(center + far_shift[...] + mixed, 0.0)
        stage[slot] = value.reshape(far_rows, size, channels)
        copy(slot, k * far_rows).start()
        return carry

    lax.fori_loop(0, count, far_step, 0)
    for k in range(max(count - 2, 0), count):
        copy(k % 2, k * far_rows).wait()


def edge_strips(frame, size):
    high = size - 2 * HALO
    channels = frame.shape[1]
    band, side = HALO * size, high * PAD
    top = frame[0:band].reshape(HALO, size, channels)
    low = frame[band : 2 * band].reshape(HALO, size, channels)
    left = frame[2 * band : 2 * band + side].reshape(high, PAD, channels)
    right = frame[2 * band + side :].reshape(high, PAD, channels)
    left = jnp.concatenate([top[:, :PAD], left, low[:, :PAD]], axis=0)
    right = jnp.concatenate([top[:, size - PAD :], right, low[:, size - PAD :]], axis=0)
    return top, low, left, right


def swap_pairs(near, far, axis):
    count = lax.axis_size(axis)

    def swap(first, value):
        pairs = [(i, i + 1) for i in range(first, count - 1, 2)]
        return lax.ppermute(value, axis, pairs + [(j, i) for i, j in pairs])

    near = swap(0, near)
    far = swap(1, far)
    return near, far


def exchange(low, high, axis):
    even = lax.axis_index(axis) % 2 == 0
    return swap_pairs(jnp.where(even, high, low), jnp.where(even, low, high), axis)


def strip_kernel(left, right, row_near, row_far, near, far, wide, dense):
    size, _, channels = left.shape
    width = row_near.shape[1]
    rows = size + 2 * HALO
    head = HALO * PAD
    even_row = lax.rem(lax.axis_index("row"), 2) == 0
    even_col = lax.rem(lax.axis_index("col"), 2) == 0

    for side, edge in enumerate((left, right)):
        columns = slice(side * (width - PAD), side * (width - PAD) + PAD)
        wide[head : head + size * PAD, :] = (
            edge[...].reshape(size * PAD, channels).astype(F32)
        )
        for even, above, below in (
            (True, row_far, row_near),
            (False, row_near, row_far),
        ):

            @pl.when(even_row if even else jnp.logical_not(even_row))
            def _(above=above, below=below, columns=columns):
                wide[0:head, :] = (
                    above[:, columns, :].reshape(head, channels).astype(F32)
                )
                wide[head + size * PAD :, :] = (
                    below[:, columns, :].reshape(head, channels).astype(F32)
                )

        for c in range(HALO):
            line = c + side * (PAD - HALO)
            dense[c * rows : (c + 1) * rows, :] = wide[pl.ds(line, rows, stride=PAD), :]

        packed = dense[...].astype(BF16)

        @pl.when(even_col)
        def _(side=side, packed=packed):
            (near if side else far)[...] = packed

        @pl.when(jnp.logical_not(even_col))
        def _(side=side, packed=packed):
            (far if side else near)[...] = packed


def halo_pieces(top, low, left, right):
    size, channels = left.shape[0], left.shape[2]
    rows = size + 2 * HALO
    row_near, row_far = exchange(top, low, "row")
    whole = pl.BlockSpec(memory_space=pltpu.VMEM)
    strip = jax.ShapeDtypeStruct((HALO * rows, channels), BF16)
    near, far = pl.pallas_call(
        strip_kernel,
        out_shape=[strip, strip],
        in_specs=[whole] * 4,
        out_specs=[whole] * 2,
        scratch_shapes=[
            pltpu.VMEM((PAD * rows, channels), F32),
            pltpu.VMEM((HALO * rows, channels), F32),
        ],
        compiler_params=pltpu.CompilerParams(vmem_limit_bytes=GRANT // 4),
    )(left, right, row_near, row_far)
    return (row_near, row_far) + swap_pairs(near, far, "col")


def compute(
    features,
    kernel_first,
    bias_first,
    mixer_first,
    shift_first,
    kernel_second,
    bias_second,
    mixer_second,
    shift_second,
):
    size, _, channels = features.shape
    count = lax.axis_size("row")
    rows = size + 2 * HALO
    width = size + 2 * PAD
    groups = (size + 2 * FAR) // (2 * NEAR)
    pair = ("row", "col")
    straight, hop, onward = mirror_routes(count)

    def send(value, route):
        return lax.ppermute(value, pair, route)

    turn = lambda part: jnp.swapaxes(part, 0, 1)
    frame = jnp.concatenate(
        [
            turn(piece).reshape(-1, channels)
            for piece in (
                features[:, :HALO],
                features[:, size - HALO :],
                features[:PAD, HALO : size - HALO],
                features[size - PAD :, HALO : size - HALO],
            )
        ],
        axis=0,
    )
    inside = turn(features[PAD : size - PAD, HALO : size - HALO])
    direct_frame = send(frame, straight + hop)
    hop_inside = send(inside, hop)
    direct = send(inside, straight)
    relayed_frame = send(direct_frame, onward)
    relayed = send(hop_inside, onward)

    row, col = lax.axis_index("row"), lax.axis_index("col")
    diagonal = row == col
    anti = row + col == count - 1
    mirror_frame = jnp.where(
        diagonal, frame, jnp.where(anti, relayed_frame, direct_frame)
    )
    own_halos = halo_pieces(
        features[:HALO],
        features[size - HALO :],
        features[:, :PAD],
        features[:, size - PAD :],
    )
    halos = halo_pieces(*edge_strips(mirror_frame, size))

    whole = pl.BlockSpec(memory_space=pltpu.VMEM)
    line = lambda v: v.reshape(1, channels)
    ext = pltpu.VMEM((rows, 2 * LEAD + size, channels), BF16)
    wide = pltpu.VMEM(
        (rows // (2 * NEAR), 2, NEAR, width, 3 * channels), BF16
    )
    lines = [
        pltpu.VMEM((PAD * rows, channels), F32),
        pltpu.VMEM((HALO * rows, channels), F32),
    ]
    field = (groups, 2, NEAR, width, channels)
    pairs = (12 * channels, 2 * channels)
    square = (2 * channels, 2 * channels)
    near_flops = 2 * groups * 2 * NEAR * width * 10 * channels * channels
    own_block = pl.pallas_call(
        functools.partial(own_kernel, steps=1),
        out_shape=[
            jax.ShapeDtypeStruct(shape, BF16)
            for shape in (field, pairs, square, pairs, square)
        ],
        in_specs=[whole] * 11,
        out_specs=[whole] * 5,
        scratch_shapes=[ext, wide, pltpu.VMEM(pairs, BF16)] + lines,
        cost_estimate=pl.CostEstimate(
            flops=2 * near_flops, bytes_accessed=8 << 20, transcendentals=0
        ),
        compiler_params=pltpu.CompilerParams(vmem_limit_bytes=GRANT),
        name="own_block",
    )
    own_operands = (
        features,
        *own_halos,
        kernel_first,
        line(bias_first),
        mixer_first,
        line(shift_first),
        kernel_second,
        mixer_second,
    )
    summed, taps, mix, far_taps, far_mix = own_block(*own_operands)

    far_rows = size // 2
    return pl.pallas_call(
        functools.partial(main_kernel, steps=1, far_rows=far_rows),
        out_shape=jax.ShapeDtypeStruct(features.shape, F32),
        in_specs=[whole] * 16,
        out_specs=pl.BlockSpec(memory_space=pl.ANY),
        scratch_shapes=[
            ext,
            wide,
            pltpu.VMEM((groups, 2, NEAR, size, 3 * channels), BF16),
            pltpu.VMEM((2, far_rows, size, channels), F32),
            pltpu.SemaphoreType.DMA((2,)),
        ]
        + lines,
        cost_estimate=pl.CostEstimate(
            flops=4 * near_flops, bytes_accessed=16 << 20, transcendentals=0
        ),
        compiler_params=pltpu.CompilerParams(vmem_limit_bytes=GRANT),
        name="main_block",
    )(
        mirror_frame,
        inside,
        direct,
        relayed,
        *halos,
        summed,
        taps,
        line(bias_first),
        mix,
        far_taps,
        line(bias_second),
        far_mix,
        line(shift_second),
    )


def solution(mesh):
    return jax.shard_map(
        compute,
        mesh=mesh,
        in_specs=(P(("groups", "row"), "col", None), P(), P(), P(), P(), P(), P(), P(), P()),
        out_specs=P(("groups", "row"), "col", None),
        check_vma=False,
    )
```
